128 devices in a mesh: pts: 32 (over z, x, core), rep: 4 (over y).
Axes of the slice: x: 4, y: 4, z: 4, core: 2. Of those that a mesh axis runs over, the one named last changes fastest.
Arguments:
- target_xyz: float32 [3, 32768], P(None, 'pts'), may hold values from 0 to 1
- source_xyz: float32 [3, 65536], P(None, ('pts', 'rep')), may hold values from 0 to 1
- target_count: int32 [32], P('pts'), may hold values from 1 to 1024, as said below
- source_count: int32 [128], P(('pts', 'rep')), may hold values from 1 to 512, as said below
- psi: bfloat16 [32768, 256], P('pts'), may hold values from -6 to 6
- omega: bfloat16 [65536, 256], P(('pts', 'rep')), may hold values from -6 to 6
Outputs:
- range_sketch: float32 [32768, 256], P('pts')
- corange_sketch: float32 [65536, 256], P(('pts', 'rep'))
- core: float32 [256, 256], replicated
- range_gram: float32 [256, 256], replicated
- corange_gram: float32 [256, 256], replicated
The draws below stay inside these ranges and needn't reach their ends.
Inputs may be any that keep to these rules, and one draw needn't show every extreme that they name: `target_count`: each group holds 1 to 1024 live targets; some group holds exactly 1024. `source_count`: each shard holds 1 to 512 live sources; some shard holds exactly 512.
All inputs are finite; a program needn't handle non-finite values.
Results may differ from the reference program's by a relative error of at most 0.0003.
The reference program's roundings to bfloat16 on the way (of `tile`) count: a program that leaves them out, or rounds other values in their place, can miss the bound.
Values may be sent and summed in bfloat16 or wider, within the bound.
No kernel may reach another device: no remote copies, remote signals or barrier semaphores. Data moves between devices by JAX's collectives and lax.ppermute only.
A program may use at most 64 MiB of HBM per device.

```python
import math
import jax
import jax.numpy as jnp
from jax import lax

R = 256
TCAP = 1024
SCAP = 512
NGROUP = 32
NSHARD = 128
TARGETS = 32768
SOURCES = 65536


def skewed_counts(key, number, capacity):
    low = max(capacity // 8, 1)
    high = max(5 * capacity // 8 + 1, low + 1)
    counts = jax.random.randint(jax.random.fold_in(key, 11), (number,), low, high, dtype=jnp.int32)
    where_full = jax.random.randint(jax.random.fold_in(key, 12), (), 0, number, dtype=jnp.int32)
    return counts.at[where_full].set(capacity)


def draw_target_count(key, part):
    return skewed_counts(jax.random.fold_in(key, 1), NGROUP, TCAP)


def draw_source_count(key, part):
    return skewed_counts(jax.random.fold_in(key, 2), NSHARD, SCAP)


def block_levels(stream_key, shape, pieces, low, high):
    def one(axis_at, parts):
        steps = jax.random.uniform(jax.random.fold_in(jax.random.fold_in(stream_key, 6), axis_at), (parts,), jnp.float32, low / len(pieces), high / len(pieces))
        return jnp.repeat(jnp.exp(steps), shape[axis_at] // parts).reshape((-1,) + (1,) * (len(shape) - axis_at - 1))

    level = one(*pieces[0])
    for cut in pieces[1:]:
        level = level * one(*cut)
    return level


def scatter_about(key, extent, deviation, bound, pieces=(), kind=jnp.bfloat16):
    loudness = block_levels(key, extent, pieces, -0.22, 0.18) if pieces else 1.0
    values = jax.random.normal(key, extent, jnp.float32) * deviation * loudness
    return jnp.minimum(jnp.maximum(values, -bound), bound).astype(kind)


def setup_inputs(seed: int = 0) -> dict:
    key_list = jax.random.split(jax.random.key(seed), 7)
    return {
        "target_xyz": jnp.clip(1.0 * jax.random.uniform(key_list[0], (3, TARGETS), jnp.float32) ** block_levels(key_list[0], (3, TARGETS), ((1, 32),), -0.2, 0.2), 0.0, 1.0),
        "source_xyz": jnp.clip(1.0 * jax.random.uniform(key_list[1], (3, SOURCES), jnp.float32) ** block_levels(key_list[1], (3, SOURCES), ((1, 128),), -0.2, 0.2), 0.0, 1.0),
        "target_count": draw_target_count(jax.random.fold_in(key_list[6], 71), 0),
        "source_count": draw_source_count(jax.random.fold_in(key_list[6], 71), 0),
        "psi": scatter_about(key_list[4], (TARGETS, R), 1.0, 6.0, ((0, 32),)),
        "omega": scatter_about(key_list[5], (SOURCES, R), 1.0, 6.0, ((0, 128),)),
    }


SHIFT = 1.05
SPREAD = 8.0

def tile_block(tgt, src):
    dx = tgt[0][:, None] - (src[0][None, :] + SHIFT)
    dy = SPREAD * (tgt[1][:, None] - src[1][None, :])
    dz = SPREAD * (tgt[2][:, None] - src[2][None, :])
    return lax.rsqrt(dx * dx + dy * dy + dz * dz).astype(jnp.bfloat16)

def reference(target_xyz, source_xyz, target_count, source_count, psi, omega):
    tslot = jnp.arange(TARGETS, dtype=jnp.int32)
    sslot = jnp.arange(SOURCES, dtype=jnp.int32)
    tlive = tslot % TCAP < target_count[tslot // TCAP]
    slive = sslot % SCAP < source_count[sslot // SCAP]
    psi_live = jnp.where(tlive[:, None], psi, jnp.zeros_like(psi))
    omega_live = jnp.where(slive[:, None], omega, jnp.zeros_like(omega))
    nblocks = SOURCES // SCAP

    def per_group(zacc, gidx):
        tgt = lax.dynamic_slice_in_dim(target_xyz, gidx * TCAP, TCAP, 1)
        prow = lax.dynamic_slice_in_dim(psi_live, gidx * TCAP, TCAP, 0)

        def per_block(carry, bidx):
            yacc, zinner = carry
            src = lax.dynamic_slice_in_dim(source_xyz, bidx * SCAP, SCAP, 1)
            orow = lax.dynamic_slice_in_dim(omega_live, bidx * SCAP, SCAP, 0)
            tile = tile_block(tgt, src)
            yacc = yacc + jnp.dot(tile, orow, preferred_element_type=jnp.float32)
            zterm = lax.dot_general(tile, prow, (((0,), (0,)), ((), ())), preferred_element_type=jnp.float32)
            old = lax.dynamic_slice_in_dim(zinner, bidx * SCAP, SCAP, 0)
            zinner = lax.dynamic_update_slice_in_dim(zinner, old + zterm, bidx * SCAP, 0)
            return ((yacc, zinner), None)
        init = (jnp.zeros((TCAP, R), jnp.float32), zacc)
        (yacc, zacc), _ = lax.scan(per_block, init, jnp.arange(nblocks, dtype=jnp.int32))
        return (zacc, yacc)
    zsum, yblocks = lax.scan(per_group, jnp.zeros((SOURCES, R), jnp.float32), jnp.arange(NGROUP, dtype=jnp.int32))
    yfull = yblocks.reshape(TARGETS, R) * (2.0 / math.sqrt(SOURCES))
    range_sketch = jnp.where(tlive[:, None], yfull, jnp.zeros_like(yfull))
    zfull = zsum * (2.0 / math.sqrt(TARGETS))
    corange_sketch = jnp.where(slive[:, None], zfull, jnp.zeros_like(zfull))
    hi = lax.Precision.HIGHEST
    core = jnp.dot(psi_live.astype(jnp.float32).T, range_sketch, precision=hi) / math.sqrt(TARGETS)
    range_gram = jnp.dot(range_sketch.T, range_sketch, precision=hi) / TARGETS
    corange_gram = jnp.dot(corange_sketch.T, corange_sketch, precision=hi) / SOURCES
    return (range_sketch, corange_sketch, core, range_gram, corange_gram)
```

```python
import math

import jax
import jax.numpy as jnp
from jax import lax
from jax.experimental import pallas as pl
from jax.experimental.pallas import tpu as pltpu
from jax.sharding import Mesh, PartitionSpec as P

SHIFT = 1.05
SPREAD = 8.0
ZN, XN, CN, YN = 4, 4, 2, 4
ALL = ("z", "x", "c", "y")
R = 256
TCAP, SCAP = 1024, 512
TQ = TCAP // YN
GRAN = 16
NT = ZN * XN
NS = CN * YN
TC = 256
SC = 512
TPAY = TQ + 32
SPAY = SCAP + 64
FAR = 4.0
F32 = jnp.float32
BF16 = jnp.bfloat16


def three_pieces(v):
    hi = v.astype(BF16)
    rest = v - hi.astype(F32)
    mid = rest.astype(BF16)
    low = (rest - mid.astype(F32)).astype(BF16)
    return hi, mid, low


def pack_kernel(where_ref, txyz_ref, sxyz_ref, psi_ref, omega_ref, tpay_ref, spay_ref, cols, quarter):
    yq = where_ref[0]
    tcount = where_ref[1]
    scount = where_ref[2]
    rows16 = lax.broadcasted_iota(jnp.int32, (GRAN, R), 0)
    cols[...] = jnp.concatenate(
        [txyz_ref[...], jnp.zeros((5, TCAP), F32)], axis=0
    ).T
    for a in range(TQ // GRAN):
        start = pl.multiple_of((a * YN + yq) * GRAN, GRAN)
        block = psi_ref[pl.ds(start, GRAN), :]
        tpay_ref[a * GRAN:(a + 1) * GRAN, :] = jnp.where(
            rows16 + start < tcount, block, jnp.zeros_like(block)
        )
        quarter[a * GRAN:(a + 1) * GRAN, :] = cols[pl.ds(start, GRAN), :]
    step = GRAN * YN
    tlive = (tcount // step) * GRAN + jnp.clip(tcount % step - yq * GRAN, 0, GRAN)
    sub = lax.broadcasted_iota(jnp.int32, (8, TQ), 0)
    tpos = quarter[...].T
    tpos = jnp.where((sub == 1) | (sub == 2), tpos * SPREAD, tpos)
    tpos = jnp.where(sub == 3, tlive.astype(F32), tpos)
    tail = jnp.zeros((8, R), BF16)
    tpay_ref[TQ:TPAY, :] = jnp.concatenate([*three_pieces(tpos), tail], axis=0)
    srow = lax.broadcasted_iota(jnp.int32, (SCAP, R), 0)
    om = omega_ref[...]
    spay_ref[0:SCAP, :] = jnp.where(srow < scount, om, jnp.zeros_like(om))
    for h in range(SCAP // R):
        part = jnp.concatenate(
            [sxyz_ref[:, h * R:(h + 1) * R], jnp.zeros((5, R), F32)], axis=0
        )
        part = jnp.where((sub == 1) | (sub == 2), part * SPREAD, part)
        part = jnp.where(sub == 0, part + SHIFT, part)
        part = jnp.where(sub == 3, (scount - h * R).clip(0, R).astype(F32), part)
        base = SCAP + 32 * h
        spay_ref[base:base + 32, :] = jnp.concatenate([*three_pieces(part), tail], axis=0)


def pack(where, txyz, sxyz, psi, omega):
    vm = pl.BlockSpec(memory_space=pltpu.VMEM)
    return pl.pallas_call(
        pack_kernel,
        out_shape=(
            jax.ShapeDtypeStruct((TPAY, R), BF16),
            jax.ShapeDtypeStruct((SPAY, R), BF16),
        ),
        in_specs=[pl.BlockSpec(memory_space=pltpu.SMEM), vm, vm, vm, vm],
        out_specs=(vm, vm),
        scratch_shapes=[pltpu.VMEM((TCAP, 8), F32), pltpu.VMEM((TQ, 8), F32)],
    )(where, txyz, sxyz, psi, omega)


def join(ref, *at):
    lo = at[-1]
    lead = at[:-1]
    v = ref[(*lead, slice(lo, lo + 32), slice(None))].astype(F32)
    return v[0:8] + v[8:16] + v[16:24]


def ceil16(n):
    return ((n + GRAN - 1) // GRAN) * GRAN


def sketch_kernel(cnt_ref, t0, t1, t2, t3, s0, s1, y0, y1, y2, y3, z0, z1,
                  psic, tpos, omc, spos, srow, bcx, bcy, bcz, yc, zc):
    tin, sin = (t0, t1, t2, t3), (s0, s1)
    youts, zouts = (y0, y1, y2, y3), (z0, z1)
    toff = [jnp.int32(0)]
    for k in range(NT):
        ref, d = tin[k // ZN], k % ZN
        off = pl.multiple_of(toff[k], GRAN)
        psic[pl.ds(off, TQ), :] = ref[d, 0:TQ, :]
        tpos[pl.ds(off, TQ), :] = join(ref, d, TQ).T
        toff.append(toff[k] + ceil16(cnt_ref[k]))
    tend = pl.multiple_of(toff[NT], GRAN)
    psic[pl.ds(tend, TC), :] = jnp.zeros((TC, R), BF16)
    tpos[pl.ds(tend, TC), :] = jnp.zeros((TC, 8), F32)
    soff = [jnp.int32(0)]
    for k in range(NS):
        ref, d = sin[k // YN], k % YN
        off = pl.multiple_of(soff[k], GRAN)
        omc[pl.ds(off, SCAP), :] = ref[d, 0:SCAP, :]
        for h in range(SCAP // R):
            spos[pl.ds(off + h * R, R), :] = join(ref, d, SCAP + 32 * h).T
        soff.append(soff[k] + ceil16(cnt_ref[NT + k]))
    send = pl.multiple_of(soff[NS], GRAN)
    omc[pl.ds(send, SC), :] = jnp.zeros((SC, R), BF16)
    spos[pl.ds(send, SC), :] = jnp.full((SC, 8), FAR, F32)
    nt = (toff[NT] + TC - 1) // TC
    ns = (soff[NS] + SC - 1) // SC

    def prepare(si, carry):
        at = pl.multiple_of(si * SC, SC)
        srow[si] = spos[pl.ds(at, SC), :].T
        zc[pl.ds(at, SC), :] = jnp.zeros((SC, R), F32)
        return carry

    lax.fori_loop(0, ns, prepare, 0)

    def over_targets(ti, carry):
        ta = pl.multiple_of(ti * TC, TC)
        tp = tpos[pl.ds(ta, TC), :]
        bcx[...] = jnp.broadcast_to(tp[:, 0:1], (TC, 128))
        bcy[...] = jnp.broadcast_to(tp[:, 1:2], (TC, 128))
        bcz[...] = jnp.broadcast_to(tp[:, 2:3], (TC, 128))
        yc[pl.ds(ta, TC), :] = jnp.zeros((TC, R), F32)

        def over_sources(si, inner):
            sa = pl.multiple_of(si * SC, SC)
            pieces = []
            for j in range(SC // 128):
                lanes = slice(j * 128, (j + 1) * 128)
                dx = bcx[...] - srow[si, 0:1, lanes]
                dy = bcy[...] - srow[si, 1:2, lanes]
                dz = bcz[...] - srow[si, 2:3, lanes]
                pieces.append(lax.rsqrt(dx * dx + dy * dy + dz * dz).astype(BF16))
            tile = jnp.concatenate(pieces, axis=1)
            yc[pl.ds(ta, TC), :] += jnp.dot(
                tile, omc[pl.ds(sa, SC), :], preferred_element_type=F32
            )
            zc[pl.ds(sa, SC), :] += lax.dot_general(
                tile, psic[pl.ds(ta, TC), :], (((0,), (0,)), ((), ())),
                preferred_element_type=F32,
            )
            return inner

        lax.fori_loop(0, ns, over_sources, 0)
        return carry

    lax.fori_loop(0, nt, over_targets, 0)
    for k in range(NT):
        off = pl.multiple_of(toff[k], GRAN)
        youts[k // ZN][k % ZN] = yc[pl.ds(off, TQ), :]
    for k in range(NS):
        off = pl.multiple_of(soff[k], GRAN)
        zouts[k // YN][k % YN] = zc[pl.ds(off, SCAP), :]


def sketch(counts, tin, sin):
    vm = pl.BlockSpec(memory_space=pltpu.VMEM)
    trows = NT * TQ + 2 * TC
    srows = NS * SCAP + 2 * SC
    return pl.pallas_call(
        sketch_kernel,
        out_shape=(
            *[jax.ShapeDtypeStruct((ZN, TQ, R), F32)] * XN,
            *[jax.ShapeDtypeStruct((YN, SCAP, R), F32)] * CN,
        ),
        in_specs=[pl.BlockSpec(memory_space=pltpu.SMEM)] + [vm] * 6,
        out_specs=(vm,) * 6,
        scratch_shapes=[
            pltpu.VMEM((trows, R), BF16),
            pltpu.VMEM((trows, 8), F32),
            pltpu.VMEM((srows, R), BF16),
            pltpu.VMEM((srows, 8), F32),
            pltpu.VMEM((srows // SC, 8, SC), F32),
            pltpu.VMEM((TC, 128), F32),
            pltpu.VMEM((TC, 128), F32),
            pltpu.VMEM((TC, 128), F32),
            pltpu.VMEM((trows, R), F32),
            pltpu.VMEM((srows, R), F32),
        ],
    )(counts, *tin, *sin)


def fetch(v, axis, d):
    n = lax.axis_size(axis)
    return lax.ppermute(v, axis, [((i + d) % n, i) for i in range(n)])


def give(v, axis, d):
    n = lax.axis_size(axis)
    return lax.ppermute(v, axis, [(i, (i + d) % n) for i in range(n)])


def local(target_xyz, source_xyz, target_count, source_count, psi, omega):
    yq = lax.axis_index("y")
    tcount, scount = target_count[0], source_count[0]
    where = jnp.stack([yq, tcount, scount]).astype(jnp.int32)
    tpay, spay = pack(where, target_xyz, source_xyz, psi, omega)
    column = jnp.stack([tpay] + [fetch(tpay, "z", d) for d in range(1, ZN)])
    srep = jnp.stack([spay] + [fetch(spay, "y", d) for d in range(1, YN)])
    tin = [column] + [fetch(column, "x", d) for d in range(1, XN)]
    sin = [srep, fetch(srep, "c", 1)]
    counts = [t[:, TQ + 3, 0].astype(jnp.int32) for t in tin]
    counts += [
        s[:, SCAP + 3, 0].astype(jnp.int32) + s[:, SCAP + 35, 0].astype(jnp.int32)
        for s in sin
    ]
    y0, y1, y2, y3, z0, z1 = sketch(jnp.concatenate(counts), tin, sin)
    zmine = z0 + give(z1, "c", 1)
    yx = y0 + give(y1, "x", 1) + give(y2, "x", 2) + give(y3, "x", 3)
    ysum = yx[0]
    for d in range(1, ZN):
        ysum = ysum + give(yx[d], "z", d)
    zsum = zmine[0]
    for d in range(1, YN):
        zsum = zsum + give(zmine[d], "y", d)
    all_targets = TCAP * NT * CN
    all_sources = SCAP * NT * NS
    rows = lax.broadcasted_iota(jnp.int32, (TQ // GRAN, GRAN, 1), 0) * (GRAN * YN)
    rows = rows + lax.broadcasted_iota(jnp.int32, (TQ // GRAN, GRAN, 1), 1) + yq * GRAN
    live = (rows < tcount).reshape(TQ, 1)
    yfin = jnp.where(live, ysum * (2.0 / math.sqrt(all_sources)), 0.0)
    slive = lax.broadcasted_iota(jnp.int32, (SCAP, 1), 0) < scount
    zfin = jnp.where(slive, zsum * (2.0 / math.sqrt(all_targets)), 0.0)
    hi = lax.Precision.HIGHEST
    psiq = tpay[0:TQ].astype(F32)
    core = jnp.dot(psiq.T, yfin, precision=hi) / math.sqrt(all_targets)
    ygram = jnp.dot(yfin.T, yfin, precision=hi) / all_targets
    zgram = jnp.dot(zfin.T, zfin, precision=hi) / all_sources
    parts = jnp.concatenate([core, ygram, zgram])
    n = ZN * XN * CN * YN
    share = parts.shape[0] // n
    mine = lax.all_to_all(parts.reshape(n, share, R), ALL, 0, 0, tiled=True).sum(0)
    grams = lax.all_to_all(
        jnp.broadcast_to(mine[None], (n, share, R)), ALL, 0, 0, tiled=True
    ).reshape(n * share, R)
    out = jnp.zeros((TQ // GRAN, YN, GRAN, R), F32)
    ypieces = [yfin] + [fetch(yfin, "y", d) for d in range(1, YN)]
    for d in range(YN):
        piece = ypieces[d].reshape(TQ // GRAN, 1, GRAN, R)
        out = lax.dynamic_update_slice(out, piece, (0, (yq + d) % YN, 0, 0))
    return (out.reshape(TCAP, R), zfin, grams[0:R], grams[R:2 * R], grams[2 * R:])


def solution(mesh):
    grid = Mesh(mesh.devices.reshape(ZN, XN, CN, YN), ALL)
    pts = ("z", "x", "c")
    return jax.shard_map(
        local,
        mesh=grid,
        in_specs=(P(None, pts), P(None, ALL), P(pts), P(ALL), P(pts, None), P(ALL, None)),
        out_specs=(P(pts, None), P(ALL, None), P(), P(), P()),
        check_vma=False,
    )
```

```python
import math

import jax
import jax.numpy as jnp
from jax import lax
from jax.experimental import pallas as pl
from jax.experimental.pallas import tpu as pltpu
from jax.sharding import Mesh, PartitionSpec as P

SHIFT = 1.05
SPREAD = 8.0
ZN, XN, CN, YN = 4, 4, 2, 4
ALL = ("z", "x", "c", "y")
R = 256
TCAP, SCAP = 1024, 512
TQ = TCAP // YN
GRAN = 16
NT = ZN * XN
NS = CN * YN
TC = 256
SC = 512
TH = TQ // 2
TPAY = TH + 32
SPAY = SCAP + 64
FAR = 4.0
F32 = jnp.float32
BF16 = jnp.bfloat16


def three_pieces(v):
    hi = v.astype(BF16)
    rest = v - hi.astype(F32)
    mid = rest.astype(BF16)
    low = (rest - mid.astype(F32)).astype(BF16)
    return hi, mid, low


def pack_kernel(where_ref, txyz_ref, sxyz_ref, psi_ref, omega_ref, apay_ref, bpay_ref, spay_ref, cols, quarter):
    yq = where_ref[0]
    tcount = where_ref[1]
    scount = where_ref[2]
    rows16 = lax.broadcasted_iota(jnp.int32, (GRAN, R), 0)
    cols[...] = jnp.concatenate(
        [txyz_ref[...], jnp.zeros((5, TCAP), F32)], axis=0
    ).T
    for a in range(TQ // GRAN):
        start = pl.multiple_of((a * YN + yq) * GRAN, GRAN)
        block = psi_ref[pl.ds(start, GRAN), :]
        half = (apay_ref, bpay_ref)[a * GRAN // TH]
        at = a * GRAN % TH
        half[at:at + GRAN, :] = jnp.where(
            rows16 + start < tcount, block, jnp.zeros_like(block)
        )
        quarter[a * GRAN:(a + 1) * GRAN, :] = cols[pl.ds(start, GRAN), :]
    step = GRAN * YN
    tlive = (tcount // step) * GRAN + jnp.clip(tcount % step - yq * GRAN, 0, GRAN)
    sub = lax.broadcasted_iota(jnp.int32, (8, TQ), 0)
    tpos = quarter[...].T
    tpos = jnp.where((sub == 1) | (sub == 2), tpos * SPREAD, tpos)
    tpos = jnp.where(sub == 3, tlive.astype(F32), tpos)
    tail = jnp.zeros((8, R), BF16)
    apay_ref[TH:TPAY, :] = jnp.concatenate([*three_pieces(tpos), tail], axis=0)
    srow = lax.broadcasted_iota(jnp.int32, (SCAP, R), 0)
    om = omega_ref[...]
    spay_ref[0:SCAP, :] = jnp.where(srow < scount, om, jnp.zeros_like(om))
    for h in range(SCAP // R):
        part = jnp.concatenate(
            [sxyz_ref[:, h * R:(h + 1) * R], jnp.zeros((5, R), F32)], axis=0
        )
        part = jnp.where((sub == 1) | (sub == 2), part * SPREAD, part)
        part = jnp.where(sub == 0, part + SHIFT, part)
        part = jnp.where(sub == 3, (scount - h * R).clip(0, R).astype(F32), part)
        base = SCAP + 32 * h
        spay_ref[base:base + 32, :] = jnp.concatenate([*three_pieces(part), tail], axis=0)


def pack(where, txyz, sxyz, psi, omega):
    vm = pl.BlockSpec(memory_space=pltpu.VMEM)
    return pl.pallas_call(
        pack_kernel,
        out_shape=(
            jax.ShapeDtypeStruct((TPAY, R), BF16),
            jax.ShapeDtypeStruct((TH, R), BF16),
            jax.ShapeDtypeStruct((SPAY, R), BF16),
        ),
        in_specs=[pl.BlockSpec(memory_space=pltpu.SMEM), vm, vm, vm, vm],
        out_specs=(vm, vm, vm),
        scratch_shapes=[pltpu.VMEM((TCAP, 8), F32), pltpu.VMEM((TQ, 8), F32)],
    )(where, txyz, sxyz, psi, omega)


def join(ref, *at):
    lo = at[-1]
    lead = at[:-1]
    v = ref[(*lead, slice(lo, lo + 32), slice(None))].astype(F32)
    return v[0:8] + v[8:16] + v[16:24]


def ceil16(n):
    return ((n + GRAN - 1) // GRAN) * GRAN


def sketch_kernel(a0, a1, a2, a3, b0, b1, b2, b3, s0, s1, ya0, ya1, ya2, ya3,
                  yb0, yb1, yb2, yb3, z0, z1, psic, tpos, omc, spos, srow,
                  bcx, bcy, bcz, yc, zc, cntv, cnts, sem):
    ain, bin_, sin = (a0, a1, a2, a3), (b0, b1, b2, b3), (s0, s1)
    yas, ybs, zouts = (ya0, ya1, ya2, ya3), (yb0, yb1, yb2, yb3), (z0, z1)
    for k in range(NT):
        cntv[k:k + 1, :] = join(ain[k // ZN], k % ZN, TH)[3:4, 0:128].astype(jnp.int32)
    for k in range(NS):
        both = [join(sin[k // YN], k % YN, SCAP + 32 * h)[3:4, 0:128] for h in range(SCAP // R)]
        cntv[NT + k:NT + k + 1, :] = sum(both).astype(jnp.int32)
    fetch_counts = pltpu.make_async_copy(cntv, cnts, sem)
    fetch_counts.start()
    fetch_counts.wait()
    toff = [jnp.int32(0)]
    for k in range(NT):
        dx, dz = k // ZN, k % ZN
        off = pl.multiple_of(toff[k], GRAN)
        psic[pl.ds(off, TH), :] = ain[dx][dz, 0:TH, :]
        psic[pl.ds(off + TH, TH), :] = bin_[dz][dx]
        tpos[pl.ds(off, TQ), :] = join(ain[dx], dz, TH).T
        toff.append(toff[k] + ceil16(cnts[k, 0]))
    tend = pl.multiple_of(toff[NT], GRAN)
    psic[pl.ds(tend, TC), :] = jnp.zeros((TC, R), BF16)
    tpos[pl.ds(tend, TC), :] = jnp.zeros((TC, 8), F32)
    soff = [jnp.int32(0)]
    for k in range(NS):
        ref, d = sin[k // YN], k % YN
        off = pl.multiple_of(soff[k], GRAN)
        omc[pl.ds(off, SCAP), :] = ref[d, 0:SCAP, :]
        for h in range(SCAP // R):
            spos[pl.ds(off + h * R, R), :] = join(ref, d, SCAP + 32 * h).T
        soff.append(soff[k] + ceil16(cnts[NT + k, 0]))
    send = pl.multiple_of(soff[NS], GRAN)
    omc[pl.ds(send, SC), :] = jnp.zeros((SC, R), BF16)
    spos[pl.ds(send, SC), :] = jnp.full((SC, 8), FAR, F32)
    nt = (toff[NT] + TC - 1) // TC
    ns = (soff[NS] + SC - 1) // SC

    def prepare(si, carry):
        at = pl.multiple_of(si * SC, SC)
        srow[si] = spos[pl.ds(at, SC), :].T
        zc[pl.ds(at, SC), :] = jnp.zeros((SC, R), F32)
        return carry

    lax.fori_loop(0, ns, prepare, 0)

    def over_targets(ti, carry):
        ta = pl.multiple_of(ti * TC, TC)
        tp = tpos[pl.ds(ta, TC), :]
        bcx[...] = jnp.broadcast_to(tp[:, 0:1], (TC, 128))
        bcy[...] = jnp.broadcast_to(tp[:, 1:2], (TC, 128))
        bcz[...] = jnp.broadcast_to(tp[:, 2:3], (TC, 128))
        yc[pl.ds(ta, TC), :] = jnp.zeros((TC, R), F32)

        def over_sources(si, inner):
            sa = pl.multiple_of(si * SC, SC)
            pieces = []
            for j in range(SC // 128):
                lanes = slice(j * 128, (j + 1) * 128)
                dx = bcx[...] - srow[si, 0:1, lanes]
                dy = bcy[...] - srow[si, 1:2, lanes]
                dz = bcz[...] - srow[si, 2:3, lanes]
                pieces.append(lax.rsqrt(dx * dx + dy * dy + dz * dz).astype(BF16))
            tile = jnp.concatenate(pieces, axis=1)
            yc[pl.ds(ta, TC), :] += jnp.dot(
                tile, omc[pl.ds(sa, SC), :], preferred_element_type=F32
            )
            zc[pl.ds(sa, SC), :] += lax.dot_general(
                tile, psic[pl.ds(ta, TC), :], (((0,), (0,)), ((), ())),
                preferred_element_type=F32,
            )
            return inner

        lax.fori_loop(0, ns, over_sources, 0)
        return carry

    lax.fori_loop(0, nt, over_targets, 0)
    for k in range(NT):
        dx, dz = k // ZN, k % ZN
        off = pl.multiple_of(toff[k], GRAN)
        yas[dx][dz] = yc[pl.ds(off, TH), :]
        ybs[dz][dx] = yc[pl.ds(off + TH, TH), :]
    for k in range(NS):
        off = pl.multiple_of(soff[k], GRAN)
        zouts[k // YN][k % YN] = zc[pl.ds(off, SCAP), :]


def sketch(ain, bin_, sin):
    vm = pl.BlockSpec(memory_space=pltpu.VMEM)
    trows = NT * TQ + 2 * TC
    srows = NS * SCAP + 2 * SC
    return pl.pallas_call(
        sketch_kernel,
        out_shape=(
            *[jax.ShapeDtypeStruct((ZN, TH, R), F32)] * (2 * XN),
            *[jax.ShapeDtypeStruct((YN, SCAP, R), F32)] * CN,
        ),
        in_specs=[vm] * 10,
        out_specs=(vm,) * 10,
        scratch_shapes=[
            pltpu.VMEM((trows, R), BF16),
            pltpu.VMEM((trows, 8), F32),
            pltpu.VMEM((srows, R), BF16),
            pltpu.VMEM((srows, 8), F32),
            pltpu.VMEM((srows // SC, 8, SC), F32),
            pltpu.VMEM((TC, 128), F32),
            pltpu.VMEM((TC, 128), F32),
            pltpu.VMEM((TC, 128), F32),
            pltpu.VMEM((trows, R), F32),
            pltpu.VMEM((srows, R), F32),
            pltpu.VMEM((NT + NS, 128), jnp.int32),
            pltpu.SMEM((NT + NS, 128), jnp.int32),
            pltpu.SemaphoreType.DMA(()),
        ],
    )(*ain, *bin_, *sin)


def finish_kernel(where_ref, a0, a1, a2, a3, b0, b1, b2, b3, z0, z1, z2, z3, pa, pb,
                  yfin_ref, zfin_ref, keep_ref, send_ref, *, yscale, zscale, tn, sn):
    yq, tcount, scount, core = where_ref[0], where_ref[1], where_ref[2], where_ref[3]
    row = lax.broadcasted_iota(jnp.int32, (TH, R), 0)
    for h, part in enumerate(((a0, a1, a2, a3), (b0, b1, b2, b3))):
        total = (part[0][...] + part[1][...]) + (part[2][...] + part[3][...])
        q = row + h * TH
        slot = (q // GRAN) * (GRAN * YN) + yq * GRAN + q % GRAN
        yfin_ref[h * TH:(h + 1) * TH, :] = jnp.where(slot < tcount, total * yscale, 0.0)
    srow = lax.broadcasted_iota(jnp.int32, (SCAP, R), 0)
    total = (z0[...] + z1[...]) + (z2[...] + z3[...])
    zfin_ref[...] = jnp.where(srow < scount, total * zscale, 0.0)
    psi = jnp.concatenate([pa[0:TH, :], pb[...]], axis=0).astype(F32)
    y, z = yfin_ref[...], zfin_ref[...]
    hi = lax.Precision.HIGHEST
    dims = (((0,), (0,)), ((), ()))
    parts = (
        lax.dot_general(psi, y, dims, precision=hi, preferred_element_type=F32) / math.sqrt(tn),
        lax.dot_general(y, y, dims, precision=hi, preferred_element_type=F32) / tn,
        lax.dot_general(z, z, dims, precision=hi, preferred_element_type=F32) / sn,
    )
    first = core == 0
    for k in range(3):
        top, low = parts[k][0:R // 2, :], parts[k][R // 2:, :]
        keep_ref[k] = jnp.where(first, top, low)
        send_ref[k] = jnp.where(first, low, top)


def finish(where, a, b, z, pa, pb):
    tn, sn = TCAP * NT * CN, SCAP * NT * NS
    vm = pl.BlockSpec(memory_space=pltpu.VMEM)
    half = jax.ShapeDtypeStruct((3, R // 2, R), F32)

    def body(*refs):
        finish_kernel(
            *refs, yscale=2.0 / math.sqrt(sn), zscale=2.0 / math.sqrt(tn), tn=tn, sn=sn
        )

    return pl.pallas_call(
        body,
        out_shape=(
            jax.ShapeDtypeStruct((TQ, R), F32),
            jax.ShapeDtypeStruct((SCAP, R), F32),
            half,
            half,
        ),
        in_specs=[pl.BlockSpec(memory_space=pltpu.SMEM)] + [vm] * 14,
        out_specs=(vm,) * 4,
    )(where, *a, *b, *z, pa, pb)


def place_kernel(where_ref, *refs):
    ys, own, other = refs[0:YN], refs[YN:YN + ZN], refs[YN + ZN]
    yout, outs = refs[YN + ZN + 1], refs[YN + ZN + 2:]
    yq, core, z = where_ref[0], where_ref[3], where_ref[4]
    for d in range(YN):
        q = lax.rem(yq + d, YN)
        for a in range(TQ // GRAN):
            at = pl.multiple_of((a * YN + q) * GRAN, GRAN)
            yout[pl.ds(at, GRAN), :] = ys[d][a * GRAN:(a + 1) * GRAN, :]
    share = R // CN // ZN
    for d in range(ZN):
        q = lax.rem(z + d, ZN)
        at = pl.multiple_of((core * ZN + q) * share, share)
        far = pl.multiple_of(((1 - core) * ZN + q) * share, share)
        for k in range(3):
            outs[k][pl.ds(at, share), :] = own[d][k]
            outs[k][pl.ds(far, share), :] = other[d, k]


def place(where, ys, own, other):
    vm = pl.BlockSpec(memory_space=pltpu.VMEM)
    return pl.pallas_call(
        place_kernel,
        out_shape=(
            jax.ShapeDtypeStruct((TCAP, R), F32),
            *[jax.ShapeDtypeStruct((R, R), F32)] * 3,
        ),
        in_specs=[pl.BlockSpec(memory_space=pltpu.SMEM)] + [vm] * (YN + ZN + 1),
        out_specs=(vm,) * 4,
    )(where, *ys, *own, other)


def fetch(v, axis, d):
    n = lax.axis_size(axis)
    return lax.ppermute(v, axis, [((i + d) % n, i) for i in range(n)])


def give(v, axis, d):
    n = lax.axis_size(axis)
    return lax.ppermute(v, axis, [(i, (i + d) % n) for i in range(n)])


def ring(v, axis):
    return [v] + [fetch(v, axis, d) for d in range(1, lax.axis_size(axis))]


def gathered_sum(v, axis):
    p = ring(v, axis)
    return (p[0] + p[2]) + (p[1] + p[3])


def returned(vs, axis):
    return [vs[0]] + [give(vs[d], axis, d) for d in range(1, len(vs))]


def local(target_xyz, source_xyz, target_count, source_count, psi, omega):
    yq, core, z = (lax.axis_index(n) for n in ("y", "c", "z"))
    where = jnp.stack([yq, target_count[0], source_count[0], core, z]).astype(jnp.int32)
    apay, bpay, spay = pack(where, target_xyz, source_xyz, psi, omega)
    ain = ring(jnp.stack(ring(apay, "z")), "x")
    bin_ = ring(jnp.stack(ring(bpay, "x")), "z")
    srep = jnp.stack(ring(spay, "y"))
    parts = sketch(ain, bin_, [srep, fetch(srep, "c", 1)])
    ya, yb, (z0, z1) = parts[0:4], parts[4:8], parts[8:10]
    zmine = z0 + give(z1, "c", 1)
    ax = returned(ya, "x")
    ax = (ax[0] + ax[1]) + (ax[2] + ax[3])
    bz = returned(yb, "z")
    bz = (bz[0] + bz[1]) + (bz[2] + bz[3])
    a = returned([ax[d] for d in range(ZN)], "z")
    b = returned([bz[d] for d in range(XN)], "x")
    zs = returned([zmine[d] for d in range(YN)], "y")
    yfin, zfin, keep, send = finish(where, a, b, zs, apay, bpay)
    ys = ring(yfin, "y")
    half = (keep + fetch(send, "c", 1)).reshape(3, ZN, R // CN // ZN, R)
    chunks = [
        lax.dynamic_index_in_dim(half, lax.rem(z + d, ZN), 1, keepdims=False)
        for d in range(ZN)
    ]
    p = returned(chunks, "z")
    mine = (p[0] + p[1]) + (p[2] + p[3])
    mine = gathered_sum(gathered_sum(mine, "x"), "y")
    own = ring(mine, "z")
    other = fetch(jnp.stack(own), "c", 1)
    y, g0, g1, g2 = place(where, ys, own, other)
    return (y, zfin, g0, g1, g2)


def solution(mesh):
    grid = Mesh(mesh.devices.reshape(ZN, XN, CN, YN), ALL)
    pts = ("z", "x", "c")
    return jax.shard_map(
        local,
        mesh=grid,
        in_specs=(P(None, pts), P(None, ALL), P(pts), P(ALL), P(pts, None), P(ALL, None)),
        out_specs=(P(pts, None), P(ALL, None), P(), P(), P()),
        check_vma=False,
    )
```

```python
import math

import jax
import jax.numpy as jnp
from jax import lax
from jax.experimental import pallas as pl
from jax.experimental.pallas import tpu as pltpu
from jax.sharding import Mesh, PartitionSpec as P


SHIFT = 1.05
SPREAD = 8.0
ZN, XN, CN, YN = 4, 4, 2, 4
ALL = ("z", "x", "c", "y")
R = 256
TCAP, SCAP = 1024, 512
TQ = TCAP // YN
GRAN = 16
NT = ZN * XN
NS = CN * YN
TC = 256
SC = 512
TH = TQ // 2
TPAY = TH + 32
SPAY = SCAP + 64
FAR = 4.0
F32 = jnp.float32
BF16 = jnp.bfloat16


def three_pieces(v):
    hi = v.astype(BF16)
    rest = v - hi.astype(F32)
    mid = rest.astype(BF16)
    low = (rest - mid.astype(F32)).astype(BF16)
    return hi, mid, low


def pack_kernel(where_ref, txyz_ref, sxyz_ref, psi_ref, omega_ref, apay_ref, bpay_ref, spay_ref, cols, quarter):
    yq = where_ref[0]
    tcount = where_ref[1]
    scount = where_ref[2]
    rows16 = lax.broadcasted_iota(jnp.int32, (GRAN, R), 0)
    cols[...] = jnp.concatenate(
        [txyz_ref[...], jnp.zeros((5, TCAP), F32)], axis=0
    ).T
    for a in range(TQ // GRAN):
        start = pl.multiple_of((a * YN + yq) * GRAN, GRAN)
        block = psi_ref[pl.ds(start, GRAN), :]
        half = (apay_ref, bpay_ref)[a * GRAN // TH]
        at = a * GRAN % TH
        half[at:at + GRAN, :] = jnp.where(
            rows16 + start < tcount, block, jnp.zeros_like(block)
        )
        quarter[a * GRAN:(a + 1) * GRAN, :] = cols[pl.ds(start, GRAN), :]
    step = GRAN * YN
    tlive = (tcount // step) * GRAN + jnp.clip(tcount % step - yq * GRAN, 0, GRAN)
    sub = lax.broadcasted_iota(jnp.int32, (8, TQ), 0)
    tpos = quarter[...].T
    tpos = jnp.where((sub == 1) | (sub == 2), tpos * SPREAD, tpos)
    tpos = jnp.where(sub == 3, tlive.astype(F32), tpos)
    tail = jnp.zeros((8, R), BF16)
    apay_ref[TH:TPAY, :] = jnp.concatenate([*three_pieces(tpos), tail], axis=0)
    srow = lax.broadcasted_iota(jnp.int32, (SCAP, R), 0)
    om = omega_ref[...]
    spay_ref[0:SCAP, :] = jnp.where(srow < scount, om, jnp.zeros_like(om))
    for h in range(SCAP // R):
        part = jnp.concatenate(
            [sxyz_ref[:, h * R:(h + 1) * R], jnp.zeros((5, R), F32)], axis=0
        )
        part = jnp.where((sub == 1) | (sub == 2), part * SPREAD, part)
        part = jnp.where(sub == 0, part + SHIFT, part)
        part = jnp.where(sub == 3, (scount - h * R).clip(0, R).astype(F32), part)
        base = SCAP + 32 * h
        spay_ref[base:base + 32, :] = jnp.concatenate([*three_pieces(part), tail], axis=0)


def pack(where, txyz, sxyz, psi, omega):
    vm = pl.BlockSpec(memory_space=pltpu.VMEM)
    return pl.pallas_call(
        pack_kernel,
        out_shape=(
            jax.ShapeDtypeStruct((TPAY, R), BF16),
            jax.ShapeDtypeStruct((TH, R), BF16),
            jax.ShapeDtypeStruct((SPAY, R), BF16),
        ),
        in_specs=[pl.BlockSpec(memory_space=pltpu.SMEM), vm, vm, vm, vm],
        out_specs=(vm, vm, vm),
        scratch_shapes=[pltpu.VMEM((TCAP, 8), F32), pltpu.VMEM((TQ, 8), F32)],
    )(where, txyz, sxyz, psi, omega)


def join(ref, *at):
    lo = at[-1]
    lead = at[:-1]
    v = ref[(*lead, slice(lo, lo + 32), slice(None))].astype(F32)
    return v[0:8] + v[8:16] + v[16:24]


def ceil16(n):
    return ((n + GRAN - 1) // GRAN) * GRAN


def sketch_kernel(a0, a1, a2, a3, b0, b1, b2, b3, s0, s1, ya0, ya1, ya2, ya3,
                  yb0, yb1, yb2, yb3, z0, z1, psic, tpos, omc, spos, srow,
                  bcx, bcy, bcz, yc, zc, cntv, cnts, sem):
    ain, bin_, sin = (a0, a1, a2, a3), (b0, b1, b2, b3), (s0, s1)
    yas, ybs, zouts = (ya0, ya1, ya2, ya3), (yb0, yb1, yb2, yb3), (z0, z1)
    for k in range(NT):
        cntv[k:k + 1, :] = join(ain[k // ZN], k % ZN, TH)[3:4, 0:128].astype(jnp.int32)
    for k in range(NS):
        both = [join(sin[k // YN], k % YN, SCAP + 32 * h)[3:4, 0:128] for h in range(SCAP // R)]
        cntv[NT + k:NT + k + 1, :] = sum(both).astype(jnp.int32)
    fetch_counts = pltpu.make_async_copy(cntv, cnts, sem)
    fetch_counts.start()
    fetch_counts.wait()
    toff = [jnp.int32(0)]
    for k in range(NT):
        dx, dz = k // ZN, k % ZN
        off = pl.multiple_of(toff[k], GRAN)
        psic[pl.ds(off, TH), :] = ain[dx][dz, 0:TH, :]
        psic[pl.ds(off + TH, TH), :] = bin_[dz][dx]
        tpos[pl.ds(off, TQ), :] = join(ain[dx], dz, TH).T
        toff.append(toff[k] + ceil16(cnts[k, 0]))
    tend = pl.multiple_of(toff[NT], GRAN)
    psic[pl.ds(tend, TC), :] = jnp.zeros((TC, R), BF16)
    tpos[pl.ds(tend, TC), :] = jnp.zeros((TC, 8), F32)
    soff = [jnp.int32(0)]
    for k in range(NS):
        ref, d = sin[k // YN], k % YN
        off = pl.multiple_of(soff[k], GRAN)
        omc[pl.ds(off, SCAP), :] = ref[d, 0:SCAP, :]
        for h in range(SCAP // R):
            spos[pl.ds(off + h * R, R), :] = join(ref, d, SCAP + 32 * h).T
        soff.append(soff[k] + ceil16(cnts[NT + k, 0]))
    send = pl.multiple_of(soff[NS], GRAN)
    omc[pl.ds(send, SC), :] = jnp.zeros((SC, R), BF16)
    spos[pl.ds(send, SC), :] = jnp.full((SC, 8), FAR, F32)
    nt = (toff[NT] + TC - 1) // TC
    ns = (soff[NS] + SC - 1) // SC

    def prepare(si, carry):
        at = pl.multiple_of(si * SC, SC)
        srow[si] = spos[pl.ds(at, SC), :].T
        zc[pl.ds(at, SC), :] = jnp.zeros((SC, R), F32)
        return carry

    lax.fori_loop(0, ns, prepare, 0)

    def over_targets(ti, carry):
        ta = pl.multiple_of(ti * TC, TC)
        tp = tpos[pl.ds(ta, TC), :]
        bcx[...] = jnp.broadcast_to(tp[:, 0:1], (TC, 128))
        bcy[...] = jnp.broadcast_to(tp[:, 1:2], (TC, 128))
        bcz[...] = jnp.broadcast_to(tp[:, 2:3], (TC, 128))
        yc[pl.ds(ta, TC), :] = jnp.zeros((TC, R), F32)

        def over_sources(si, inner):
            sa = pl.multiple_of(si * SC, SC)
            pieces = []
            for j in range(SC // 128):
                lanes = slice(j * 128, (j + 1) * 128)
                dx = bcx[...] - srow[si, 0:1, lanes]
                dy = bcy[...] - srow[si, 1:2, lanes]
                dz = bcz[...] - srow[si, 2:3, lanes]
                pieces.append(lax.rsqrt(dx * dx + dy * dy + dz * dz).astype(BF16))
            tile = jnp.concatenate(pieces, axis=1)
            yc[pl.ds(ta, TC), :] += jnp.dot(
                tile, omc[pl.ds(sa, SC), :], preferred_element_type=F32
            )
            zc[pl.ds(sa, SC), :] += lax.dot_general(
                tile, psic[pl.ds(ta, TC), :], (((0,), (0,)), ((), ())),
                preferred_element_type=F32,
            )
            return inner

        lax.fori_loop(0, ns, over_sources, 0)
        return carry

    lax.fori_loop(0, nt, over_targets, 0)
    for k in range(NT):
        dx, dz = k // ZN, k % ZN
        off = pl.multiple_of(toff[k], GRAN)
        yas[dx][dz] = yc[pl.ds(off, TH), :]
        ybs[dz][dx] = yc[pl.ds(off + TH, TH), :]
    for k in range(NS):
        off = pl.multiple_of(soff[k], GRAN)
        zouts[k // YN][k % YN] = zc[pl.ds(off, SCAP), :]


def sketch(ain, bin_, sin):
    vm = pl.BlockSpec(memory_space=pltpu.VMEM)
    trows = NT * TQ + 2 * TC
    srows = NS * SCAP + 2 * SC
    return pl.pallas_call(
        sketch_kernel,
        out_shape=(
            *[jax.ShapeDtypeStruct((ZN, TH, R), F32)] * (2 * XN),
            *[jax.ShapeDtypeStruct((YN, SCAP, R), F32)] * CN,
        ),
        in_specs=[vm] * 10,
        out_specs=(vm,) * 10,
        scratch_shapes=[
            pltpu.VMEM((trows, R), BF16),
            pltpu.VMEM((trows, 8), F32),
            pltpu.VMEM((srows, R), BF16),
            pltpu.VMEM((srows, 8), F32),
            pltpu.VMEM((srows // SC, 8, SC), F32),
            pltpu.VMEM((TC, 128), F32),
            pltpu.VMEM((TC, 128), F32),
            pltpu.VMEM((TC, 128), F32),
            pltpu.VMEM((trows, R), F32),
            pltpu.VMEM((srows, R), F32),
            pltpu.VMEM((NT + NS, 128), jnp.int32),
            pltpu.SMEM((NT + NS, 128), jnp.int32),
            pltpu.SemaphoreType.DMA(()),
        ],
    )(*ain, *bin_, *sin)


def finish_kernel(where_ref, a0, a1, a2, a3, b0, b1, b2, b3, z0, z1, z2, z3, pa, pb,
                  yfin_ref, zfin_ref, keep_ref, send_ref, *, yscale, zscale, tn, sn):
    yq, tcount, scount, core = where_ref[0], where_ref[1], where_ref[2], where_ref[3]
    row = lax.broadcasted_iota(jnp.int32, (TH, R), 0)
    for h, part in enumerate(((a0, a1, a2, a3), (b0, b1, b2, b3))):
        total = (part[0][...] + part[1][...]) + (part[2][...] + part[3][...])
        q = row + h * TH
        slot = (q // GRAN) * (GRAN * YN) + yq * GRAN + q % GRAN
        yfin_ref[h * TH:(h + 1) * TH, :] = jnp.where(slot < tcount, total * yscale, 0.0)
    srow = lax.broadcasted_iota(jnp.int32, (SCAP, R), 0)
    total = (z0[...] + z1[...]) + (z2[...] + z3[...])
    zfin_ref[...] = jnp.where(srow < scount, total * zscale, 0.0)
    psi = jnp.concatenate([pa[0:TH, :], pb[...]], axis=0).astype(F32)
    y, z = yfin_ref[...], zfin_ref[...]
    hi = lax.Precision.HIGHEST
    dims = (((0,), (0,)), ((), ()))
    parts = (
        lax.dot_general(psi, y, dims, precision=hi, preferred_element_type=F32) / math.sqrt(tn),
        lax.dot_general(y, y, dims, precision=hi, preferred_element_type=F32) / tn,
        lax.dot_general(z, z, dims, precision=hi, preferred_element_type=F32) / sn,
    )
    first = core == 0
    for k in range(3):
        top, low = parts[k][0:R // 2, :], parts[k][R // 2:, :]
        keep_ref[k] = jnp.where(first, top, low)
        send_ref[k] = jnp.where(first, low, top)


def finish(where, a, b, z, pa, pb):
    tn, sn = TCAP * NT * CN, SCAP * NT * NS
    vm = pl.BlockSpec(memory_space=pltpu.VMEM)
    half = jax.ShapeDtypeStruct((3, R // 2, R), F32)

    def body(*refs):
        finish_kernel(
            *refs, yscale=2.0 / math.sqrt(sn), zscale=2.0 / math.sqrt(tn), tn=tn, sn=sn
        )

    return pl.pallas_call(
        body,
        out_shape=(
            jax.ShapeDtypeStruct((TQ, R), F32),
            jax.ShapeDtypeStruct((SCAP, R), F32),
            half,
            half,
        ),
        in_specs=[pl.BlockSpec(memory_space=pltpu.SMEM)] + [vm] * 14,
        out_specs=(vm,) * 4,
    )(where, *a, *b, *z, pa, pb)


def place_kernel(where_ref, *refs):
    ys, own, other = refs[0:YN], refs[YN:YN + ZN], refs[YN + ZN]
    yout, outs = refs[YN + ZN + 1], refs[YN + ZN + 2:]
    yq, core, z = where_ref[0], where_ref[3], where_ref[4]
    for d in range(YN):
        q = lax.rem(yq + d, YN)
        for a in range(TQ // GRAN):
            at = pl.multiple_of((a * YN + q) * GRAN, GRAN)
            yout[pl.ds(at, GRAN), :] = ys[d][a * GRAN:(a + 1) * GRAN, :]
    share = R // CN // ZN
    for d in range(ZN):
        q = lax.rem(z + d, ZN)
        at = pl.multiple_of((core * ZN + q) * share, share)
        far = pl.multiple_of(((1 - core) * ZN + q) * share, share)
        for k in range(3):
            outs[k][pl.ds(at, share), :] = own[d][k]
            outs[k][pl.ds(far, share), :] = other[d, k]


def place(where, ys, own, other):
    vm = pl.BlockSpec(memory_space=pltpu.VMEM)
    return pl.pallas_call(
        place_kernel,
        out_shape=(
            jax.ShapeDtypeStruct((TCAP, R), F32),
            *[jax.ShapeDtypeStruct((R, R), F32)] * 3,
        ),
        in_specs=[pl.BlockSpec(memory_space=pltpu.SMEM)] + [vm] * (YN + ZN + 1),
        out_specs=(vm,) * 4,
    )(where, *ys, *own, other)


def fetch(v, axis, d):
    n = lax.axis_size(axis)
    return lax.ppermute(v, axis, [((i + d) % n, i) for i in range(n)])


def give(v, axis, d):
    n = lax.axis_size(axis)
    return lax.ppermute(v, axis, [(i, (i + d) % n) for i in range(n)])


def ring(v, axis):
    return [v] + [fetch(v, axis, d) for d in range(1, lax.axis_size(axis))]


def gathered_sum(v, axis):
    p = ring(v, axis)
    return (p[0] + p[2]) + (p[1] + p[3])


def returned(vs, axis):
    return [vs[0]] + [give(vs[d], axis, d) for d in range(1, len(vs))]


def steps(target_xyz, source_xyz, target_count, source_count, psi, omega):
    yq, core, z = (lax.axis_index(n) for n in ("y", "c", "z"))
    where = jnp.stack([yq, target_count[0], source_count[0], core, z]).astype(jnp.int32)
    apay, bpay, spay = pack(where, target_xyz, source_xyz, psi, omega)
    arow = ring(apay, "z")
    brow = ring(bpay, "x")
    srow = ring(spay, "y")
    ain = ring(jnp.stack(arow), "x")
    bin_ = ring(jnp.stack(brow), "z")
    srep = jnp.stack(srow)
    sfar = fetch(srep, "c", 1)
    parts = sketch(ain, bin_, [srep, sfar])
    ya, yb, (z0, z1) = parts[0:4], parts[4:8], parts[8:10]
    zfar = give(z1, "c", 1)
    ax = returned(ya, "x")
    bz = returned(yb, "z")
    zmine = [z0[d] + zfar[d] for d in range(YN)]
    zs = returned(zmine, "y")
    ax = [(ax[0][d] + ax[1][d]) + (ax[2][d] + ax[3][d]) for d in range(ZN)]
    bz = [(bz[0][d] + bz[1][d]) + (bz[2][d] + bz[3][d]) for d in range(XN)]
    a = returned(ax, "z")
    b = returned(bz, "x")
    yfin, zfin, keep, send = finish(where, a, b, zs, apay, bpay)
    ys = ring(yfin, "y")
    half = keep + fetch(send, "c", 1)
    half = half.reshape(3, ZN, R // CN // ZN, R)
    chunks = [
        lax.dynamic_index_in_dim(half, lax.rem(z + d, ZN), 1, keepdims=False)
        for d in range(ZN)
    ]
    p = returned(chunks, "z")
    mine = (p[0] + p[1]) + (p[2] + p[3])
    mine = gathered_sum(gathered_sum(mine, "x"), "y")
    own = ring(mine, "z")
    other = fetch(jnp.stack(own), "c", 1)
    y, g0, g1, g2 = place(where, ys, own, other)
    return (y, zfin, g0, g1, g2)


def solution(mesh):
    grid = Mesh(mesh.devices.reshape(ZN, XN, CN, YN), ALL)
    pts = ("z", "x", "c")
    return jax.shard_map(
        steps,
        mesh=grid,
        in_specs=(P(None, pts), P(None, ALL), P(pts), P(ALL), P(pts, None), P(ALL, None)),
        out_specs=(P(pts, None), P(ALL, None), P(), P(), P()),
        check_vma=False,
    )
```

```python
import math

import jax
import jax.numpy as jnp
from jax import lax
from jax.experimental import pallas as pl
from jax.experimental.pallas import tpu as pltpu
from jax.sharding import Mesh, PartitionSpec as P


SHIFT = 1.05
SPREAD = 8.0
ZN, XN, CN, YN = 4, 4, 2, 4
ALL = ("z", "x", "c", "y")
R = 256
TCAP, SCAP = 1024, 512
TQ = TCAP // YN
GRAN = 16
NT = ZN * XN
NS = CN * YN
TC = 256
SC = 512
TH = TQ // 2
TPAY = TH + 32
SPAY = SCAP + 64
FAR = 4.0
F32 = jnp.float32
BF16 = jnp.bfloat16


def inside(*arrays):
    return [pltpu.with_memory_space_constraint(v, pltpu.VMEM) for v in arrays]


def three_pieces(v):
    hi = v.astype(BF16)
    rest = v - hi.astype(F32)
    mid = rest.astype(BF16)
    low = (rest - mid.astype(F32)).astype(BF16)
    return hi, mid, low


def pack_kernel(where_ref, txyz_ref, sxyz_ref, psi_ref, omega_ref, apay_ref, bpay_ref, spay_ref, cols, quarter):
    yq = where_ref[0]
    tcount = where_ref[1]
    scount = where_ref[2]
    rows16 = lax.broadcasted_iota(jnp.int32, (GRAN, R), 0)
    cols[...] = jnp.concatenate(
        [txyz_ref[...], jnp.zeros((5, TCAP), F32)], axis=0
    ).T
    for a in range(TQ // GRAN):
        start = pl.multiple_of((a * YN + yq) * GRAN, GRAN)
        block = psi_ref[pl.ds(start, GRAN), :]
        half = (apay_ref, bpay_ref)[a * GRAN // TH]
        at = a * GRAN % TH
        half[at:at + GRAN, :] = jnp.where(
            rows16 + start < tcount, block, jnp.zeros_like(block)
        )
        quarter[a * GRAN:(a + 1) * GRAN, :] = cols[pl.ds(start, GRAN), :]
    step = GRAN * YN
    tlive = (tcount // step) * GRAN + jnp.clip(tcount % step - yq * GRAN, 0, GRAN)
    sub = lax.broadcasted_iota(jnp.int32, (8, TQ), 0)
    tpos = quarter[...].T
    tpos = jnp.where((sub == 1) | (sub == 2), tpos * SPREAD, tpos)
    tpos = jnp.where(sub == 3, tlive.astype(F32), tpos)
    tail = jnp.zeros((8, R), BF16)
    apay_ref[TH:TPAY, :] = jnp.concatenate([*three_pieces(tpos), tail], axis=0)
    srow = lax.broadcasted_iota(jnp.int32, (SCAP, R), 0)
    om = omega_ref[...]
    spay_ref[0:SCAP, :] = jnp.where(srow < scount, om, jnp.zeros_like(om))
    for h in range(SCAP // R):
        part = jnp.concatenate(
            [sxyz_ref[:, h * R:(h + 1) * R], jnp.zeros((5, R), F32)], axis=0
        )
        part = jnp.where((sub == 1) | (sub == 2), part * SPREAD, part)
        part = jnp.where(sub == 0, part + SHIFT, part)
        part = jnp.where(sub == 3, (scount - h * R).clip(0, R).astype(F32), part)
        base = SCAP + 32 * h
        spay_ref[base:base + 32, :] = jnp.concatenate([*three_pieces(part), tail], axis=0)


def pack(where, txyz, sxyz, psi, omega):
    vm = pl.BlockSpec(memory_space=pltpu.VMEM)
    return pl.pallas_call(
        pack_kernel,
        out_shape=(
            jax.ShapeDtypeStruct((TPAY, R), BF16),
            jax.ShapeDtypeStruct((TH, R), BF16),
            jax.ShapeDtypeStruct((SPAY, R), BF16),
        ),
        in_specs=[pl.BlockSpec(memory_space=pltpu.SMEM), vm, vm, vm, vm],
        out_specs=(vm, vm, vm),
        scratch_shapes=[pltpu.VMEM((TCAP, 8), F32), pltpu.VMEM((TQ, 8), F32)],
        compiler_params=pltpu.CompilerParams(vmem_limit_bytes=8 << 20),
    )(where, txyz, sxyz, psi, omega)


def join(ref, *at):
    lo = at[-1]
    lead = at[:-1]
    v = ref[(*lead, slice(lo, lo + 32), slice(None))].astype(F32)
    return v[0:8] + v[8:16] + v[16:24]


def ceil16(n):
    return ((n + GRAN - 1) // GRAN) * GRAN


def sketch_kernel(a0, a1, a2, a3, b0, b1, b2, b3, s0, s1, ya0, ya1, ya2, ya3,
                  yb0, yb1, yb2, yb3, z0, z1, psic, tpos, omc, spos, srow,
                  bcx, bcy, bcz, yc, zc, tile0, tile1, cntv, cnts, sem):
    ain, bin_, sin = (a0, a1, a2, a3), (b0, b1, b2, b3), (s0, s1)
    yas, ybs, zouts = (ya0, ya1, ya2, ya3), (yb0, yb1, yb2, yb3), (z0, z1)
    for k in range(NT):
        cntv[k:k + 1, :] = join(ain[k // ZN], k % ZN, TH)[3:4, 0:128].astype(jnp.int32)
    for k in range(NS):
        both = [join(sin[k // YN], k % YN, SCAP + 32 * h)[3:4, 0:128] for h in range(SCAP // R)]
        cntv[NT + k:NT + k + 1, :] = sum(both).astype(jnp.int32)
    fetch_counts = pltpu.make_async_copy(cntv, cnts, sem)
    fetch_counts.start()
    fetch_counts.wait()
    toff = [jnp.int32(0)]
    for k in range(NT):
        dx, dz = k // ZN, k % ZN
        off = pl.multiple_of(toff[k], GRAN)
        psic[pl.ds(off, TH), :] = ain[dx][dz, 0:TH, :]
        psic[pl.ds(off + TH, TH), :] = bin_[dz][dx]
        tpos[pl.ds(off, TQ), :] = join(ain[dx], dz, TH).T
        toff.append(toff[k] + ceil16(cnts[k, 0]))
    tend = pl.multiple_of(toff[NT], GRAN)
    psic[pl.ds(tend, 2 * TC), :] = jnp.zeros((2 * TC, R), BF16)
    tpos[pl.ds(tend, 2 * TC), :] = jnp.zeros((2 * TC, 8), F32)
    soff = [jnp.int32(0)]
    for k in range(NS):
        ref, d = sin[k // YN], k % YN
        off = pl.multiple_of(soff[k], GRAN)
        omc[pl.ds(off, SCAP), :] = ref[d, 0:SCAP, :]
        for h in range(SCAP // R):
            spos[pl.ds(off + h * R, R), :] = join(ref, d, SCAP + 32 * h).T
        soff.append(soff[k] + ceil16(cnts[NT + k, 0]))
    send = pl.multiple_of(soff[NS], GRAN)
    omc[pl.ds(send, SC), :] = jnp.zeros((SC, R), BF16)
    spos[pl.ds(send, SC), :] = jnp.full((SC, 8), FAR, F32)
    nt = (toff[NT] + TC - 1) // TC
    ns = (soff[NS] + SC - 1) // SC

    def prepare(si, carry):
        at = pl.multiple_of(si * SC, SC)
        srow[si] = spos[pl.ds(at, SC), :].T
        zc[pl.ds(at, SC), :] = jnp.zeros((SC, R), F32)
        return carry

    lax.fori_loop(0, ns, prepare, 0)

    def columns(ti, carry):
        ta = pl.multiple_of(ti * TC, TC)
        tp = tpos[pl.ds(ta, TC), :]
        bcx[ti] = jnp.broadcast_to(tp[:, 0:1], (TC, 128))
        bcy[ti] = jnp.broadcast_to(tp[:, 1:2], (TC, 128))
        bcz[ti] = jnp.broadcast_to(tp[:, 2:3], (TC, 128))
        yc[pl.ds(ta, TC), :] = jnp.zeros((TC, R), F32)
        return carry

    lax.fori_loop(0, nt + 1, columns, 0)

    def make(at, tile):
        ti, si = at
        for j in range(SC // 128):
            lanes = slice(j * 128, (j + 1) * 128)
            dx = bcx[ti] - srow[si, 0:1, lanes]
            dy = bcy[ti] - srow[si, 1:2, lanes]
            dz = bcz[ti] - srow[si, 2:3, lanes]
            tile[:, lanes] = lax.rsqrt(dx * dx + dy * dy + dz * dz).astype(BF16)

    def use(at, tile):
        ta = pl.multiple_of(at[0] * TC, TC)
        sa = pl.multiple_of(at[1] * SC, SC)
        block = tile[...]
        yc[pl.ds(ta, TC), :] += jnp.dot(
            block, omc[pl.ds(sa, SC), :], preferred_element_type=F32
        )
        zc[pl.ds(sa, SC), :] += lax.dot_general(
            block, psic[pl.ds(ta, TC), :], (((0,), (0,)), ((), ())),
            preferred_element_type=F32,
        )

    def after(at):
        wrap = at[1] + 1 == ns
        return jnp.where(wrap, at[0] + 1, at[0]), jnp.where(wrap, 0, at[1] + 1)

    start = (jnp.int32(0), jnp.int32(0))
    make(start, tile0)

    def two_steps(p, first):
        second = after(first)
        use(first, tile0)
        make(second, tile1)
        third = after(second)
        use(second, tile1)
        make(third, tile0)
        return third

    lax.fori_loop(0, (nt * ns + 1) // 2, two_steps, start)
    for k in range(NT):
        dx, dz = k // ZN, k % ZN
        off = pl.multiple_of(toff[k], GRAN)
        yas[dx][dz] = yc[pl.ds(off, TH), :]
        ybs[dz][dx] = yc[pl.ds(off + TH, TH), :]
    for k in range(NS):
        off = pl.multiple_of(soff[k], GRAN)
        zouts[k // YN][k % YN] = zc[pl.ds(off, SCAP), :]


def sketch(ain, bin_, sin):
    vm = pl.BlockSpec(memory_space=pltpu.VMEM)
    trows = NT * TQ + 2 * TC
    srows = NS * SCAP + 2 * SC
    return pl.pallas_call(
        sketch_kernel,
        out_shape=(
            *[jax.ShapeDtypeStruct((ZN, TH, R), F32)] * (2 * XN),
            *[jax.ShapeDtypeStruct((YN, SCAP, R), F32)] * CN,
        ),
        in_specs=[vm] * 10,
        out_specs=(vm,) * 10,
        scratch_shapes=[
            pltpu.VMEM((trows, R), BF16),
            pltpu.VMEM((trows, 8), F32),
            pltpu.VMEM((srows, R), BF16),
            pltpu.VMEM((srows, 8), F32),
            pltpu.VMEM((srows // SC, 8, SC), F32),
            pltpu.VMEM((trows // TC, TC, 128), F32),
            pltpu.VMEM((trows // TC, TC, 128), F32),
            pltpu.VMEM((trows // TC, TC, 128), F32),
            pltpu.VMEM((trows, R), F32),
            pltpu.VMEM((srows, R), F32),
            pltpu.VMEM((TC, SC), BF16),
            pltpu.VMEM((TC, SC), BF16),
            pltpu.VMEM((NT + NS, 128), jnp.int32),
            pltpu.SMEM((NT + NS, 128), jnp.int32),
            pltpu.SemaphoreType.DMA(()),
        ],
        compiler_params=pltpu.CompilerParams(vmem_limit_bytes=34 << 20),
    )(*inside(*ain, *bin_, *sin))


def finish_kernel(where_ref, a0, a1, a2, a3, b0, b1, b2, b3, z0, z1, z2, z3, pa, pb,
                  yfin_ref, zfin_ref, keep_ref, send_ref, *, yscale, zscale, tn, sn):
    yq, tcount, scount, core = where_ref[0], where_ref[1], where_ref[2], where_ref[3]
    row = lax.broadcasted_iota(jnp.int32, (TH, R), 0)
    for h, part in enumerate(((a0, a1, a2, a3), (b0, b1, b2, b3))):
        total = (part[0][...] + part[1][...]) + (part[2][...] + part[3][...])
        q = row + h * TH
        slot = (q // GRAN) * (GRAN * YN) + yq * GRAN + q % GRAN
        yfin_ref[h * TH:(h + 1) * TH, :] = jnp.where(slot < tcount, total * yscale, 0.0)
    srow = lax.broadcasted_iota(jnp.int32, (SCAP, R), 0)
    total = (z0[...] + z1[...]) + (z2[...] + z3[...])
    zfin_ref[...] = jnp.where(srow < scount, total * zscale, 0.0)
    psi = jnp.concatenate([pa[0:TH, :], pb[...]], axis=0).astype(F32)
    y, z = yfin_ref[...], zfin_ref[...]
    hi = lax.Precision.HIGHEST
    dims = (((0,), (0,)), ((), ()))
    parts = (
        lax.dot_general(psi, y, dims, precision=hi, preferred_element_type=F32) / math.sqrt(tn),
        lax.dot_general(y, y, dims, precision=hi, preferred_element_type=F32) / tn,
        lax.dot_general(z, z, dims, precision=hi, preferred_element_type=F32) / sn,
    )
    first = core == 0
    for k in range(3):
        top, low = parts[k][0:R // 2, :], parts[k][R // 2:, :]
        keep_ref[k] = jnp.where(first, top, low)
        send_ref[k] = jnp.where(first, low, top)


def finish(where, a, b, z, pa, pb):
    tn, sn = TCAP * NT * CN, SCAP * NT * NS
    vm = pl.BlockSpec(memory_space=pltpu.VMEM)
    half = jax.ShapeDtypeStruct((3, R // 2, R), F32)

    def body(*refs):
        finish_kernel(
            *refs, yscale=2.0 / math.sqrt(sn), zscale=2.0 / math.sqrt(tn), tn=tn, sn=sn
        )

    return pl.pallas_call(
        body,
        out_shape=(
            jax.ShapeDtypeStruct((TQ, R), F32),
            jax.ShapeDtypeStruct((SCAP, R), F32),
            half,
            half,
        ),
        in_specs=[pl.BlockSpec(memory_space=pltpu.SMEM)] + [vm] * 14,
        out_specs=(vm,) * 4,
        compiler_params=pltpu.CompilerParams(vmem_limit_bytes=14 << 20),
    )(where, *inside(*a, *b, *z, pa, pb))


def place_kernel(where_ref, *refs):
    ys, own, other = refs[0:YN], refs[YN:YN + ZN], refs[YN + ZN]
    yout, outs = refs[YN + ZN + 1], refs[YN + ZN + 2:]
    yq, core, z = where_ref[0], where_ref[3], where_ref[4]
    for d in range(YN):
        q = lax.rem(yq + d, YN)
        for a in range(TQ // GRAN):
            at = pl.multiple_of((a * YN + q) * GRAN, GRAN)
            yout[pl.ds(at, GRAN), :] = ys[d][a * GRAN:(a + 1) * GRAN, :]
    share = R // CN // ZN
    for d in range(ZN):
        q = lax.rem(z + d, ZN)
        at = pl.multiple_of((core * ZN + q) * share, share)
        far = pl.multiple_of(((1 - core) * ZN + q) * share, share)
        for k in range(3):
            outs[k][pl.ds(at, share), :] = own[d][k]
            outs[k][pl.ds(far, share), :] = other[d, k]


def place(where, ys, own, other):
    vm = pl.BlockSpec(memory_space=pltpu.VMEM)
    return pl.pallas_call(
        place_kernel,
        out_shape=(
            jax.ShapeDtypeStruct((TCAP, R), F32),
            *[jax.ShapeDtypeStruct((R, R), F32)] * 3,
        ),
        in_specs=[pl.BlockSpec(memory_space=pltpu.SMEM)] + [vm] * (YN + ZN + 1),
        out_specs=(vm,) * 4,
        compiler_params=pltpu.CompilerParams(vmem_limit_bytes=10 << 20),
    )(where, *inside(*ys, *own, other))


def fetch(v, axis, d):
    n = lax.axis_size(axis)
    return lax.ppermute(v, axis, [((i + d) % n, i) for i in range(n)])


def give(v, axis, d):
    n = lax.axis_size(axis)
    return lax.ppermute(v, axis, [(i, (i + d) % n) for i in range(n)])


def ring(v, axis):
    return [v] + [fetch(v, axis, d) for d in range(1, lax.axis_size(axis))]


def gathered_sum(v, axis):
    p = ring(v, axis)
    return (p[0] + p[2]) + (p[1] + p[3])


def returned(vs, axis):
    return [vs[0]] + [give(vs[d], axis, d) for d in range(1, len(vs))]


def steps(target_xyz, source_xyz, target_count, source_count, psi, omega):
    yq, core, z = (lax.axis_index(n) for n in ("y", "c", "z"))
    where = jnp.stack([yq, target_count[0], source_count[0], core, z]).astype(jnp.int32)
    apay, bpay, spay = pack(where, target_xyz, source_xyz, psi, omega)
    arow = ring(apay, "z")
    brow = ring(bpay, "x")
    srow = ring(spay, "y")
    ain = ring(jnp.stack(arow), "x")
    bin_ = ring(jnp.stack(brow), "z")
    srep = jnp.stack(srow)
    sfar = fetch(srep, "c", 1)
    parts = sketch(ain, bin_, [srep, sfar])
    ya, yb, (z0, z1) = parts[0:4], parts[4:8], parts[8:10]
    zfar = give(z1, "c", 1)
    ax = returned(ya, "x")
    bz = returned(yb, "z")
    zmine = [z0[d] + zfar[d] for d in range(YN)]
    zs = returned(zmine, "y")
    ax = [(ax[0][d] + ax[1][d]) + (ax[2][d] + ax[3][d]) for d in range(ZN)]
    bz = [(bz[0][d] + bz[1][d]) + (bz[2][d] + bz[3][d]) for d in range(XN)]
    a = returned(ax, "z")
    b = returned(bz, "x")
    yfin, zfin, keep, send = finish(where, a, b, zs, apay, bpay)
    ys = ring(yfin, "y")
    half = keep + fetch(send, "c", 1)
    half = half.reshape(3, ZN, R // CN // ZN, R)
    chunks = [
        lax.dynamic_index_in_dim(half, lax.rem(z + d, ZN), 1, keepdims=False)
        for d in range(ZN)
    ]
    p = returned(chunks, "z")
    mine = (p[0] + p[1]) + (p[2] + p[3])
    mine = gathered_sum(gathered_sum(mine, "x"), "y")
    own = ring(mine, "z")
    other = fetch(jnp.stack(own), "c", 1)
    y, g0, g1, g2 = place(where, ys, own, other)
    return (y, zfin, g0, g1, g2)


def solution(mesh):
    grid = Mesh(mesh.devices.reshape(ZN, XN, CN, YN), ALL)
    pts = ("z", "x", "c")
    return jax.shard_map(
        steps,
        mesh=grid,
        in_specs=(P(None, pts), P(None, ALL), P(pts), P(ALL), P(pts, None), P(ALL, None)),
        out_specs=(P(pts, None), P(ALL, None), P(), P(), P()),
        check_vma=False,
    )
```

```python
import math

import jax
import jax.numpy as jnp
from jax import lax
from jax.experimental import pallas as pl
from jax.experimental.pallas import tpu as pltpu
from jax.sharding import Mesh, PartitionSpec as P


SHIFT = 1.05
SPREAD = 8.0
ZN, XN, CN, YN = 4, 4, 2, 4
ALL = ("z", "x", "c", "y")
R = 256
TCAP, SCAP = 1024, 512
TQ = TCAP // YN
GRAN = 16
NT = ZN * XN
NS = CN * YN
TC = 256
SC = 512
TPAY = TQ + 32
SPAY = SCAP + 64
FAR = 4.0
F32 = jnp.float32
BF16 = jnp.bfloat16


def inside(*arrays):
    return [pltpu.with_memory_space_constraint(v, pltpu.VMEM) for v in arrays]


def three_pieces(v):
    hi = v.astype(BF16)
    rest = v - hi.astype(F32)
    mid = rest.astype(BF16)
    low = (rest - mid.astype(F32)).astype(BF16)
    return hi, mid, low


def pack_kernel(where_ref, txyz_ref, sxyz_ref, psi_ref, omega_ref, tpay_ref, spay_ref, cols, quarter):
    yq = where_ref[0]
    tcount = where_ref[1]
    scount = where_ref[2]
    rows16 = lax.broadcasted_iota(jnp.int32, (GRAN, R), 0)
    cols[...] = jnp.concatenate(
        [txyz_ref[...], jnp.zeros((5, TCAP), F32)], axis=0
    ).T
    for a in range(TQ // GRAN):
        start = pl.multiple_of((a * YN + yq) * GRAN, GRAN)
        block = psi_ref[pl.ds(start, GRAN), :]
        tpay_ref[a * GRAN:(a + 1) * GRAN, :] = jnp.where(
            rows16 + start < tcount, block, jnp.zeros_like(block)
        )
        quarter[a * GRAN:(a + 1) * GRAN, :] = cols[pl.ds(start, GRAN), :]
    step = GRAN * YN
    tlive = (tcount // step) * GRAN + jnp.clip(tcount % step - yq * GRAN, 0, GRAN)
    sub = lax.broadcasted_iota(jnp.int32, (8, TQ), 0)
    tpos = quarter[...].T
    tpos = jnp.where((sub == 1) | (sub == 2), tpos * SPREAD, tpos)
    tpos = jnp.where(sub == 3, tlive.astype(F32), tpos)
    tail = jnp.zeros((8, R), BF16)
    tpay_ref[TQ:TPAY, :] = jnp.concatenate([*three_pieces(tpos), tail], axis=0)
    srow = lax.broadcasted_iota(jnp.int32, (SCAP, R), 0)
    om = omega_ref[...]
    spay_ref[0:SCAP, :] = jnp.where(srow < scount, om, jnp.zeros_like(om))
    for h in range(SCAP // R):
        part = jnp.concatenate(
            [sxyz_ref[:, h * R:(h + 1) * R], jnp.zeros((5, R), F32)], axis=0
        )
        part = jnp.where((sub == 1) | (sub == 2), part * SPREAD, part)
        part = jnp.where(sub == 0, part + SHIFT, part)
        part = jnp.where(sub == 3, (scount - h * R).clip(0, R).astype(F32), part)
        base = SCAP + 32 * h
        spay_ref[base:base + 32, :] = jnp.concatenate([*three_pieces(part), tail], axis=0)


def pack(where, txyz, sxyz, psi, omega):
    vm = pl.BlockSpec(memory_space=pltpu.VMEM)
    return pl.pallas_call(
        pack_kernel,
        out_shape=(
            jax.ShapeDtypeStruct((TPAY, R), BF16),
            jax.ShapeDtypeStruct((SPAY, R), BF16),
        ),
        in_specs=[pl.BlockSpec(memory_space=pltpu.SMEM), vm, vm, vm, vm],
        out_specs=(vm, vm),
        scratch_shapes=[pltpu.VMEM((TCAP, 8), F32), pltpu.VMEM((TQ, 8), F32)],
    )(where, txyz, sxyz, psi, omega)


def join(ref, *at):
    lo = at[-1]
    lead = at[:-1]
    v = ref[(*lead, slice(lo, lo + 32), slice(None))].astype(F32)
    return v[0:8] + v[8:16] + v[16:24]


def ceil16(n):
    return ((n + GRAN - 1) // GRAN) * GRAN


def sketch_kernel(t0, t1, t2, t3, s0, s1, y0, y1, y2, y3, z0, z1, psic, tpos, omc, spos, srow,
                  bcx, bcy, bcz, yc, zc, tile0, tile1, cntv, cnts, sem):
    tin, sin = (t0, t1, t2, t3), (s0, s1)
    youts, zouts = (y0, y1, y2, y3), (z0, z1)
    for k in range(NT):
        cntv[k:k + 1, :] = join(tin[k // ZN], k % ZN, TQ)[3:4, 0:128].astype(jnp.int32)
    for k in range(NS):
        both = [join(sin[k // YN], k % YN, SCAP + 32 * h)[3:4, 0:128] for h in range(SCAP // R)]
        cntv[NT + k:NT + k + 1, :] = sum(both).astype(jnp.int32)
    fetch_counts = pltpu.make_async_copy(cntv, cnts, sem)
    fetch_counts.start()
    fetch_counts.wait()
    toff = [jnp.int32(0)]
    for k in range(NT):
        ref, d = tin[k // ZN], k % ZN
        off = pl.multiple_of(toff[k], GRAN)
        psic[pl.ds(off, TQ), :] = ref[d, 0:TQ, :]
        tpos[pl.ds(off, TQ), :] = join(ref, d, TQ).T
        toff.append(toff[k] + ceil16(cnts[k, 0]))
    tend = pl.multiple_of(toff[NT], GRAN)
    psic[pl.ds(tend, 2 * TC), :] = jnp.zeros((2 * TC, R), BF16)
    tpos[pl.ds(tend, 2 * TC), :] = jnp.zeros((2 * TC, 8), F32)
    soff = [jnp.int32(0)]
    for k in range(NS):
        ref, d = sin[k // YN], k % YN
        off = pl.multiple_of(soff[k], GRAN)
        omc[pl.ds(off, SCAP), :] = ref[d, 0:SCAP, :]
        for h in range(SCAP // R):
            spos[pl.ds(off + h * R, R), :] = join(ref, d, SCAP + 32 * h).T
        soff.append(soff[k] + ceil16(cnts[NT + k, 0]))
    send = pl.multiple_of(soff[NS], GRAN)
    omc[pl.ds(send, SC), :] = jnp.zeros((SC, R), BF16)
    spos[pl.ds(send, SC), :] = jnp.full((SC, 8), FAR, F32)
    nt = (toff[NT] + TC - 1) // TC
    ns = (soff[NS] + SC - 1) // SC

    def prepare(si, carry):
        at = pl.multiple_of(si * SC, SC)
        srow[si] = spos[pl.ds(at, SC), :].T
        zc[pl.ds(at, SC), :] = jnp.zeros((SC, R), F32)
        return carry

    lax.fori_loop(0, ns, prepare, 0)

    def columns(ti, carry):
        ta = pl.multiple_of(ti * TC, TC)
        tp = tpos[pl.ds(ta, TC), :]
        bcx[ti] = jnp.broadcast_to(tp[:, 0:1], (TC, 128))
        bcy[ti] = jnp.broadcast_to(tp[:, 1:2], (TC, 128))
        bcz[ti] = jnp.broadcast_to(tp[:, 2:3], (TC, 128))
        yc[pl.ds(ta, TC), :] = jnp.zeros((TC, R), F32)
        return carry

    lax.fori_loop(0, nt + 1, columns, 0)

    def make(at, tile):
        ti, si = at
        for j in range(SC // 128):
            lanes = slice(j * 128, (j + 1) * 128)
            dx = bcx[ti] - srow[si, 0:1, lanes]
            dy = bcy[ti] - srow[si, 1:2, lanes]
            dz = bcz[ti] - srow[si, 2:3, lanes]
            tile[:, lanes] = lax.rsqrt(dx * dx + dy * dy + dz * dz).astype(BF16)

    def use(at, tile):
        ta = pl.multiple_of(at[0] * TC, TC)
        sa = pl.multiple_of(at[1] * SC, SC)
        block = tile[...]
        yc[pl.ds(ta, TC), :] += jnp.dot(
            block, omc[pl.ds(sa, SC), :], preferred_element_type=F32
        )
        zc[pl.ds(sa, SC), :] += lax.dot_general(
            block, psic[pl.ds(ta, TC), :], (((0,), (0,)), ((), ())),
            preferred_element_type=F32,
        )

    def after(at):
        wrap = at[1] + 1 == ns
        return jnp.where(wrap, at[0] + 1, at[0]), jnp.where(wrap, 0, at[1] + 1)

    start = (jnp.int32(0), jnp.int32(0))
    make(start, tile0)

    def two_steps(p, first):
        second = after(first)
        use(first, tile0)
        make(second, tile1)
        third = after(second)
        use(second, tile1)
        make(third, tile0)
        return third

    lax.fori_loop(0, (nt * ns + 1) // 2, two_steps, start)
    for k in range(NT):
        off = pl.multiple_of(toff[k], GRAN)
        youts[k // ZN][k % ZN] = yc[pl.ds(off, TQ), :]
    for k in range(NS):
        off = pl.multiple_of(soff[k], GRAN)
        zouts[k // YN][k % YN] = zc[pl.ds(off, SCAP), :]


def sketch(tin, sin):
    vm = pl.BlockSpec(memory_space=pltpu.VMEM)
    trows = NT * TQ + 2 * TC
    srows = NS * SCAP + 2 * SC
    return pl.pallas_call(
        sketch_kernel,
        out_shape=(
            *[jax.ShapeDtypeStruct((ZN, TQ, R), F32)] * XN,
            *[jax.ShapeDtypeStruct((YN, SCAP, R), F32)] * CN,
        ),
        in_specs=[vm] * 6,
        out_specs=(vm,) * 6,
        scratch_shapes=[
            pltpu.VMEM((trows, R), BF16),
            pltpu.VMEM((trows, 8), F32),
            pltpu.VMEM((srows, R), BF16),
            pltpu.VMEM((srows, 8), F32),
            pltpu.VMEM((srows // SC, 8, SC), F32),
            pltpu.VMEM((trows // TC, TC, 128), F32),
            pltpu.VMEM((trows // TC, TC, 128), F32),
            pltpu.VMEM((trows // TC, TC, 128), F32),
            pltpu.VMEM((trows, R), F32),
            pltpu.VMEM((srows, R), F32),
            pltpu.VMEM((TC, SC), BF16),
            pltpu.VMEM((TC, SC), BF16),
            pltpu.VMEM((NT + NS, 128), jnp.int32),
            pltpu.SMEM((NT + NS, 128), jnp.int32),
            pltpu.SemaphoreType.DMA(()),
        ],
        compiler_params=pltpu.CompilerParams(vmem_limit_bytes=34 << 20),
    )(*inside(*tin, *sin))


def finish_kernel(where_ref, y0, y1, y2, y3, z0, z1, z2, z3, tpay,
                  yfin_ref, zfin_ref, keep_ref, send_ref, *, yscale, zscale, tn, sn):
    yq, tcount, scount, core = where_ref[0], where_ref[1], where_ref[2], where_ref[3]
    q = lax.broadcasted_iota(jnp.int32, (TQ, R), 0)
    slot = (q // GRAN) * (GRAN * YN) + yq * GRAN + q % GRAN
    total = (y0[...] + y1[...]) + (y2[...] + y3[...])
    yfin_ref[...] = jnp.where(slot < tcount, total * yscale, 0.0)
    srow = lax.broadcasted_iota(jnp.int32, (SCAP, R), 0)
    total = (z0[...] + z1[...]) + (z2[...] + z3[...])
    zfin_ref[...] = jnp.where(srow < scount, total * zscale, 0.0)
    psi = tpay[0:TQ, :].astype(F32)
    y, z = yfin_ref[...], zfin_ref[...]
    hi = lax.Precision.HIGHEST
    dims = (((0,), (0,)), ((), ()))
    parts = (
        lax.dot_general(psi, y, dims, precision=hi, preferred_element_type=F32) / math.sqrt(tn),
        lax.dot_general(y, y, dims, precision=hi, preferred_element_type=F32) / tn,
        lax.dot_general(z, z, dims, precision=hi, preferred_element_type=F32) / sn,
    )
    first = core == 0
    for k in range(3):
        top, low = parts[k][0:R // 2, :], parts[k][R // 2:, :]
        keep_ref[k] = jnp.where(first, top, low)
        send_ref[k] = jnp.where(first, low, top)


def finish(where, y, z, tpay):
    tn, sn = TCAP * NT * CN, SCAP * NT * NS
    vm = pl.BlockSpec(memory_space=pltpu.VMEM)
    half = jax.ShapeDtypeStruct((3, R // 2, R), F32)

    def body(*refs):
        finish_kernel(
            *refs, yscale=2.0 / math.sqrt(sn), zscale=2.0 / math.sqrt(tn), tn=tn, sn=sn
        )

    return pl.pallas_call(
        body,
        out_shape=(
            jax.ShapeDtypeStruct((TQ, R), F32),
            jax.ShapeDtypeStruct((SCAP, R), F32),
            half,
            half,
        ),
        in_specs=[pl.BlockSpec(memory_space=pltpu.SMEM)] + [vm] * 9,
        out_specs=(vm,) * 4,
        compiler_params=pltpu.CompilerParams(vmem_limit_bytes=14 << 20),
    )(where, *inside(*y, *z, tpay))


def place_kernel(where_ref, *refs):
    ys, own, other = refs[0:YN], refs[YN:YN + ZN], refs[YN + ZN]
    yout, outs = refs[YN + ZN + 1], refs[YN + ZN + 2:]
    yq, core = where_ref[0], where_ref[3]
    for d in range(YN):
        q = lax.rem(yq + d, YN)
        for a in range(TQ // GRAN):
            at = pl.multiple_of((a * YN + q) * GRAN, GRAN)
            yout[pl.ds(at, GRAN), :] = ys[d][a * GRAN:(a + 1) * GRAN, :]
    share = R // CN // ZN
    for d in range(ZN):
        q = lax.rem(where_ref[4] + d, ZN)
        at = pl.multiple_of((core * ZN + q) * share, share)
        q = lax.rem(where_ref[5] + d, ZN)
        far = pl.multiple_of(((1 - core) * ZN + q) * share, share)
        for k in range(3):
            outs[k][pl.ds(at, share), :] = own[d][k]
            outs[k][pl.ds(far, share), :] = other[d, k]


def place(where, ys, own, other):
    vm = pl.BlockSpec(memory_space=pltpu.VMEM)
    return pl.pallas_call(
        place_kernel,
        out_shape=(
            jax.ShapeDtypeStruct((TCAP, R), F32),
            *[jax.ShapeDtypeStruct((R, R), F32)] * 3,
        ),
        in_specs=[pl.BlockSpec(memory_space=pltpu.SMEM)] + [vm] * (YN + ZN + 1),
        out_specs=(vm,) * 4,
        compiler_params=pltpu.CompilerParams(vmem_limit_bytes=10 << 20),
    )(where, *inside(*ys, *own, other))


FIRST = ("x", "z")
LAST = ("z", "x")
SAME = {name: (name, name) for name in ALL}


def shifted(axes, d):
    pairs = []
    size = dict(z=ZN, x=XN, c=CN, y=YN)
    for z in range(ZN):
        for x in range(XN):
            for c in range(CN):
                for y in range(YN):
                    at = dict(z=z, x=x, c=c, y=y)
                    to = dict(at)
                    to[axes[c]] = (at[axes[c]] + d) % size[axes[c]]
                    flat = [((p["z"] * XN + p["x"]) * CN + p["c"]) * YN + p["y"] for p in (at, to)]
                    pairs.append(tuple(flat))
    return pairs


def fetch(v, axes, d):
    return lax.ppermute(v, ALL, [(b, a) for a, b in shifted(axes, d)])


def give(v, axes, d):
    return lax.ppermute(v, ALL, shifted(axes, d))


def ring(v, axes):
    return [v] + [fetch(v, axes, d) for d in range(1, 4)]


def gathered_sum(v, axes):
    p = ring(v, axes)
    return (p[0] + p[2]) + (p[1] + p[3])


def returned(vs, axes):
    return [vs[0]] + [give(vs[d], axes, d) for d in range(1, len(vs))]


def steps(target_xyz, source_xyz, target_count, source_count, psi, omega):
    z, x, core, yq = (lax.axis_index(n) for n in ALL)
    along = jnp.where(core == 0, x, z)
    across = jnp.where(core == 0, z, x)
    where = jnp.stack([yq, target_count[0], source_count[0], core, along, across])
    where = where.astype(jnp.int32)
    tpay, spay = pack(where, target_xyz, source_xyz, psi, omega)
    trow = ring(tpay, FIRST)
    srow = ring(spay, SAME["y"])
    tin = ring(jnp.stack(trow), LAST)
    srep = jnp.stack(srow)
    sfar = fetch(srep, SAME["c"], 1)
    parts = sketch(tin, [srep, sfar])
    ys, (z0, z1) = parts[0:4], parts[4:6]
    zfar = give(z1, SAME["c"], 1)
    ys = returned(ys, LAST)
    zmine = [z0[d] + zfar[d] for d in range(YN)]
    zs = returned(zmine, SAME["y"])
    ys = [(ys[0][d] + ys[1][d]) + (ys[2][d] + ys[3][d]) for d in range(ZN)]
    ys = returned(ys, FIRST)
    yfin, zfin, keep, send = finish(where, ys, zs, tpay)
    ys = ring(yfin, SAME["y"])
    half = keep + fetch(send, SAME["c"], 1)
    half = half.reshape(3, ZN, R // CN // ZN, R)
    chunks = [
        lax.dynamic_index_in_dim(half, lax.rem(along + d, ZN), 1, keepdims=False)
        for d in range(ZN)
    ]
    p = returned(chunks, FIRST)
    mine = (p[0] + p[1]) + (p[2] + p[3])
    mine = gathered_sum(gathered_sum(mine, LAST), SAME["y"])
    own = ring(mine, FIRST)
    other = fetch(jnp.stack(own), SAME["c"], 1)
    y, g0, g1, g2 = place(where, ys, own, other)
    return (y, zfin, g0, g1, g2)


def solution(mesh):
    grid = Mesh(mesh.devices.reshape(ZN, XN, CN, YN), ALL)
    pts = ("z", "x", "c")
    return jax.shard_map(
        steps,
        mesh=grid,
        in_specs=(P(None, pts), P(None, ALL), P(pts), P(ALL), P(pts, None), P(ALL, None)),
        out_specs=(P(pts, None), P(ALL, None), P(), P(), P()),
        check_vma=False,
    )
```

```python
import functools
import math

import jax
import jax.numpy as jnp
from jax import lax
from jax.experimental import pallas as pl
from jax.experimental.pallas import tpu as pltpu
from jax.sharding import Mesh, PartitionSpec as P


SHIFT = 1.05
SPREAD = 8.0
ZN, XN, CN, YN = 4, 4, 2, 4
ALL = ("z", "x", "c", "y")
R = 256
TCAP, SCAP = 1024, 512
TQ = TCAP // YN
GRAN = 16
NT = ZN * XN
NS = CN * YN
TC = 256
SC = 512
TPAY = TQ + 32
SPAY = SCAP + 64
FAR = 4.0
F32 = jnp.float32
BF16 = jnp.bfloat16


def inside(*arrays):
    return [pltpu.with_memory_space_constraint(v, pltpu.VMEM) for v in arrays]


def three_pieces(v):
    hi = v.astype(BF16)
    rest = v - hi.astype(F32)
    mid = rest.astype(BF16)
    low = (rest - mid.astype(F32)).astype(BF16)
    return hi, mid, low


def pack_kernel(where_ref, txyz_ref, sxyz_ref, psi_ref, omega_ref, tpay_ref, spay_ref, cols, quarter):
    yq = where_ref[0]
    tcount = where_ref[1]
    scount = where_ref[2]
    rows16 = lax.broadcasted_iota(jnp.int32, (GRAN, R), 0)
    cols[...] = jnp.concatenate(
        [txyz_ref[...], jnp.zeros((5, TCAP), F32)], axis=0
    ).T
    for a in range(TQ // GRAN):
        start = pl.multiple_of((a * YN + yq) * GRAN, GRAN)
        block = psi_ref[pl.ds(start, GRAN), :]
        tpay_ref[a * GRAN:(a + 1) * GRAN, :] = jnp.where(
            rows16 + start < tcount, block, jnp.zeros_like(block)
        )
        quarter[a * GRAN:(a + 1) * GRAN, :] = cols[pl.ds(start, GRAN), :]
    step = GRAN * YN
    tlive = (tcount // step) * GRAN + jnp.clip(tcount % step - yq * GRAN, 0, GRAN)
    sub = lax.broadcasted_iota(jnp.int32, (8, TQ), 0)
    tpos = quarter[...].T
    tpos = jnp.where((sub == 1) | (sub == 2), tpos * SPREAD, tpos)
    tpos = jnp.where(sub == 3, tlive.astype(F32), tpos)
    tail = jnp.zeros((8, R), BF16)
    tpay_ref[TQ:TPAY, :] = jnp.concatenate([*three_pieces(tpos), tail], axis=0)
    srow = lax.broadcasted_iota(jnp.int32, (SCAP, R), 0)
    om = omega_ref[...]
    spay_ref[0:SCAP, :] = jnp.where(srow < scount, om, jnp.zeros_like(om))
    for h in range(SCAP // R):
        part = jnp.concatenate(
            [sxyz_ref[:, h * R:(h + 1) * R], jnp.zeros((5, R), F32)], axis=0
        )
        part = jnp.where((sub == 1) | (sub == 2), part * SPREAD, part)
        part = jnp.where(sub == 0, part + SHIFT, part)
        part = jnp.where(sub == 3, (scount - h * R).clip(0, R).astype(F32), part)
        base = SCAP + 32 * h
        spay_ref[base:base + 32, :] = jnp.concatenate([*three_pieces(part), tail], axis=0)


def pack(where, txyz, sxyz, psi, omega):
    vm = pl.BlockSpec(memory_space=pltpu.VMEM)
    return pl.pallas_call(
        pack_kernel,
        out_shape=(
            jax.ShapeDtypeStruct((TPAY, R), BF16),
            jax.ShapeDtypeStruct((SPAY, R), BF16),
        ),
        in_specs=[pl.BlockSpec(memory_space=pltpu.SMEM), vm, vm, vm, vm],
        out_specs=(vm, vm),
        scratch_shapes=[pltpu.VMEM((TCAP, 8), F32), pltpu.VMEM((TQ, 8), F32)],
    )(where, txyz, sxyz, psi, omega)


def join(ref, *at):
    lo = at[-1]
    lead = at[:-1]
    v = ref[(*lead, slice(lo, lo + 32), slice(None))].astype(F32)
    return v[0:8] + v[8:16] + v[16:24]


def ceil16(n):
    return ((n + GRAN - 1) // GRAN) * GRAN


TROWS = 2 * TC
SROWS = NS * SCAP + 2 * SC


def spread_counts(cntv, cnts, sem):
    copy = pltpu.make_async_copy(cntv, cnts, sem)
    copy.start()
    copy.wait()


def offsets(cnts, first, number):
    off = [jnp.int32(0)]
    for k in range(number):
        off.append(off[k] + ceil16(cnts[first + k, 0]))
    return [pl.multiple_of(v, GRAN) for v in off]


def sources_kernel(s0, s1, omc, srow, scnt, spos, cnts, sem):
    sin = (s0, s1)
    for k in range(NS):
        both = [join(sin[k // YN], k % YN, SCAP + 32 * h)[3:4, 0:128] for h in range(SCAP // R)]
        scnt[k:k + 1, :] = sum(both).astype(jnp.int32)
    spread_counts(scnt, cnts, sem)
    soff = offsets(cnts, 0, NS)
    for k in range(NS):
        ref, d = sin[k // YN], k % YN
        omc[pl.ds(soff[k], SCAP), :] = ref[d, 0:SCAP, :]
        for h in range(SCAP // R):
            spos[pl.ds(soff[k] + h * R, R), :] = join(ref, d, SCAP + 32 * h).T
    omc[pl.ds(soff[NS], SC), :] = jnp.zeros((SC, R), BF16)
    spos[pl.ds(soff[NS], SC), :] = jnp.full((SC, 8), FAR, F32)

    def prepare(si, carry):
        srow[si] = spos[pl.ds(pl.multiple_of(si * SC, SC), SC), :].T
        return carry

    lax.fori_loop(0, (soff[NS] + SC - 1) // SC, prepare, 0)


def sources(sin):
    vm = pl.BlockSpec(memory_space=pltpu.VMEM)
    return pl.pallas_call(
        sources_kernel,
        out_shape=(
            jax.ShapeDtypeStruct((SROWS, R), BF16),
            jax.ShapeDtypeStruct((SROWS // SC, 8, SC), F32),
            jax.ShapeDtypeStruct((NS, 128), jnp.int32),
        ),
        in_specs=[vm] * 2,
        out_specs=(vm,) * 3,
        scratch_shapes=[
            pltpu.VMEM((SROWS, 8), F32),
            pltpu.SMEM((NS, 128), jnp.int32),
            pltpu.SemaphoreType.DMA(()),
        ],
        compiler_params=pltpu.CompilerParams(vmem_limit_bytes=5 << 20),
    )(*inside(*sin))


def sketch_kernel(m, last, *refs):
    groups = m * ZN
    tin, refs = refs[:m], refs[m:]
    omc, srow, scnt = refs[:3]
    refs = refs[3:]
    if last:
        earlier, refs = refs[:2], refs[2:]
    youts, refs = refs[:m], refs[m:]
    if last:
        zouts, refs = refs[:2], refs[2:]
        (psic, tpos, bcx, bcy, bcz, yc, tile0, tile1, cntv, cnts, sem, zc) = refs
    else:
        zc = refs[0]
        (psic, tpos, bcx, bcy, bcz, yc, tile0, tile1, cntv, cnts, sem) = refs[1:]
    cntv[0:NS, :] = scnt[...]
    for k in range(groups):
        count = join(tin[k // ZN], k % ZN, TQ)[3:4, 0:128]
        cntv[NS + k:NS + k + 1, :] = count.astype(jnp.int32)
    spread_counts(cntv, cnts, sem)
    soff = offsets(cnts, 0, NS)
    toff = offsets(cnts, NS, groups)
    for k in range(groups):
        ref, d = tin[k // ZN], k % ZN
        psic[pl.ds(toff[k], TQ), :] = ref[d, 0:TQ, :]
        tpos[pl.ds(toff[k], TQ), :] = join(ref, d, TQ).T
    psic[pl.ds(toff[groups], 2 * TC), :] = jnp.zeros((2 * TC, R), BF16)
    tpos[pl.ds(toff[groups], 2 * TC), :] = jnp.zeros((2 * TC, 8), F32)
    nt = (toff[groups] + TC - 1) // TC
    ns = (soff[NS] + SC - 1) // SC

    def clear(si, carry):
        zc[pl.ds(pl.multiple_of(si * SC, SC), SC), :] = jnp.zeros((SC, R), F32)
        return carry

    lax.fori_loop(0, ns, clear, 0)

    def columns(ti, carry):
        ta = pl.multiple_of(ti * TC, TC)
        tp = tpos[pl.ds(ta, TC), :]
        bcx[ti] = jnp.broadcast_to(tp[:, 0:1], (TC, 128))
        bcy[ti] = jnp.broadcast_to(tp[:, 1:2], (TC, 128))
        bcz[ti] = jnp.broadcast_to(tp[:, 2:3], (TC, 128))
        yc[pl.ds(ta, TC), :] = jnp.zeros((TC, R), F32)
        return carry

    lax.fori_loop(0, nt + 1, columns, 0)

    def make(at, tile):
        ti, si = at
        for j in range(SC // 128):
            lanes = slice(j * 128, (j + 1) * 128)
            dx = bcx[ti] - srow[si, 0:1, lanes]
            dy = bcy[ti] - srow[si, 1:2, lanes]
            dz = bcz[ti] - srow[si, 2:3, lanes]
            tile[:, lanes] = lax.rsqrt(dx * dx + dy * dy + dz * dz).astype(BF16)

    def use(at, tile):
        ta = pl.multiple_of(at[0] * TC, TC)
        sa = pl.multiple_of(at[1] * SC, SC)
        block = tile[...]
        yc[pl.ds(ta, TC), :] += jnp.dot(
            block, omc[pl.ds(sa, SC), :], preferred_element_type=F32
        )
        zc[pl.ds(sa, SC), :] += lax.dot_general(
            block, psic[pl.ds(ta, TC), :], (((0,), (0,)), ((), ())),
            preferred_element_type=F32,
        )

    def after(at):
        wrap = at[1] + 1 == ns
        return jnp.where(wrap, at[0] + 1, at[0]), jnp.where(wrap, 0, at[1] + 1)

    start = (jnp.int32(0), jnp.int32(0))
    make(start, tile0)

    def two_steps(p, first):
        second = after(first)
        use(first, tile0)
        make(second, tile1)
        third = after(second)
        use(second, tile1)
        make(third, tile0)
        return third

    lax.fori_loop(0, (nt * ns + 1) // 2, two_steps, start)
    for k in range(groups):
        youts[k // ZN][k % ZN] = yc[pl.ds(toff[k], TQ), :]
    if last:
        for k in range(NS):
            rows = pl.ds(soff[k], SCAP)
            total = zc[rows, :] + (earlier[0][rows, :] + earlier[1][rows, :])
            zouts[k // YN][k % YN] = total


def sketch(tin, src, earlier=None):
    m = len(tin)
    last = earlier is not None
    vm = pl.BlockSpec(memory_space=pltpu.VMEM)
    trows = m * ZN * TQ + TROWS
    ypart = jax.ShapeDtypeStruct((ZN, TQ, R), F32)
    zhalf = jax.ShapeDtypeStruct((YN, SCAP, R), F32)
    zall = (SROWS, R)
    outs = [ypart] * m + ([zhalf] * CN if last else [jax.ShapeDtypeStruct(zall, F32)])
    operands = [*tin, *src, *(earlier or ())]
    column = pltpu.VMEM((trows // TC, TC, 128), F32)
    scratch = [
        pltpu.VMEM((trows, R), BF16),
        pltpu.VMEM((trows, 8), F32),
        column,
        column,
        column,
        pltpu.VMEM((trows, R), F32),
        pltpu.VMEM((TC, SC), BF16),
        pltpu.VMEM((TC, SC), BF16),
        pltpu.VMEM((NS + m * ZN + 8 - m * ZN % 8, 128), jnp.int32),
        pltpu.SMEM((NS + m * ZN + 8 - m * ZN % 8, 128), jnp.int32),
        pltpu.SemaphoreType.DMA(()),
    ]
    return pl.pallas_call(
        functools.partial(sketch_kernel, m, last),
        out_shape=tuple(outs),
        in_specs=[vm] * len(operands),
        out_specs=(vm,) * len(outs),
        scratch_shapes=scratch + ([pltpu.VMEM(zall, F32)] if last else []),
        compiler_params=pltpu.CompilerParams(vmem_limit_bytes=(8 + 5 * m + 6 * last) << 20),
    )(*inside(*operands))


def finish_kernel(where_ref, y0, y1, y2, y3, z0, z1, z2, z3, tpay,
                  yfin_ref, zfin_ref, keep_ref, send_ref, *, yscale, zscale, tn, sn):
    yq, tcount, scount, core = where_ref[0], where_ref[1], where_ref[2], where_ref[3]
    q = lax.broadcasted_iota(jnp.int32, (TQ, R), 0)
    slot = (q // GRAN) * (GRAN * YN) + yq * GRAN + q % GRAN
    total = (y0[...] + y1[...]) + (y2[...] + y3[...])
    yfin_ref[...] = jnp.where(slot < tcount, total * yscale, 0.0)
    srow = lax.broadcasted_iota(jnp.int32, (SCAP, R), 0)
    total = (z0[...] + z1[...]) + (z2[...] + z3[...])
    zfin_ref[...] = jnp.where(srow < scount, total * zscale, 0.0)
    psi = tpay[0:TQ, :].astype(F32)
    y, z = yfin_ref[...], zfin_ref[...]
    hi = lax.Precision.HIGHEST
    dims = (((0,), (0,)), ((), ()))
    parts = (
        lax.dot_general(psi, y, dims, precision=hi, preferred_element_type=F32) / math.sqrt(tn),
        lax.dot_general(y, y, dims, precision=hi, preferred_element_type=F32) / tn,
        lax.dot_general(z, z, dims, precision=hi, preferred_element_type=F32) / sn,
    )
    first = core == 0
    for k in range(3):
        top, low = parts[k][0:R // 2, :], parts[k][R // 2:, :]
        keep_ref[k] = jnp.where(first, top, low)
        send_ref[k] = jnp.where(first, low, top)


def finish(where, y, z, tpay):
    tn, sn = TCAP * NT * CN, SCAP * NT * NS
    vm = pl.BlockSpec(memory_space=pltpu.VMEM)
    half = jax.ShapeDtypeStruct((3, R // 2, R), F32)

    def body(*refs):
        finish_kernel(
            *refs, yscale=2.0 / math.sqrt(sn), zscale=2.0 / math.sqrt(tn), tn=tn, sn=sn
        )

    return pl.pallas_call(
        body,
        out_shape=(
            jax.ShapeDtypeStruct((TQ, R), F32),
            jax.ShapeDtypeStruct((SCAP, R), F32),
            half,
            half,
        ),
        in_specs=[pl.BlockSpec(memory_space=pltpu.SMEM)] + [vm] * 9,
        out_specs=(vm,) * 4,
        compiler_params=pltpu.CompilerParams(vmem_limit_bytes=14 << 20),
    )(where, *inside(*y, *z, tpay))


def place_kernel(where_ref, *refs):
    ys, own, other = refs[0:YN], refs[YN:YN + ZN], refs[YN + ZN]
    yout, outs = refs[YN + ZN + 1], refs[YN + ZN + 2:]
    yq, core = where_ref[0], where_ref[3]
    for d in range(YN):
        q = lax.rem(yq + d, YN)
        for a in range(TQ // GRAN):
            at = pl.multiple_of((a * YN + q) * GRAN, GRAN)
            yout[pl.ds(at, GRAN), :] = ys[d][a * GRAN:(a + 1) * GRAN, :]
    share = R // CN // ZN
    for d in range(ZN):
        q = lax.rem(where_ref[4] + d, ZN)
        at = pl.multiple_of((core * ZN + q) * share, share)
        q = lax.rem(where_ref[5] + d, ZN)
        far = pl.multiple_of(((1 - core) * ZN + q) * share, share)
        for k in range(3):
            outs[k][pl.ds(at, share), :] = own[d][k]
            outs[k][pl.ds(far, share), :] = other[d, k]


def place(where, ys, own, other):
    vm = pl.BlockSpec(memory_space=pltpu.VMEM)
    return pl.pallas_call(
        place_kernel,
        out_shape=(
            jax.ShapeDtypeStruct((TCAP, R), F32),
            *[jax.ShapeDtypeStruct((R, R), F32)] * 3,
        ),
        in_specs=[pl.BlockSpec(memory_space=pltpu.SMEM)] + [vm] * (YN + ZN + 1),
        out_specs=(vm,) * 4,
        compiler_params=pltpu.CompilerParams(vmem_limit_bytes=10 << 20),
    )(where, *inside(*ys, *own, other))


FIRST = ("x", "z")
LAST = ("z", "x")
SAME = {name: (name, name) for name in ALL}


def shifted(axes, d):
    pairs = []
    size = dict(z=ZN, x=XN, c=CN, y=YN)
    for z in range(ZN):
        for x in range(XN):
            for c in range(CN):
                for y in range(YN):
                    at = dict(z=z, x=x, c=c, y=y)
                    to = dict(at)
                    to[axes[c]] = (at[axes[c]] + d) % size[axes[c]]
                    flat = [((p["z"] * XN + p["x"]) * CN + p["c"]) * YN + p["y"] for p in (at, to)]
                    pairs.append(tuple(flat))
    return pairs


def fetch(v, axes, d):
    return lax.ppermute(v, ALL, [(b, a) for a, b in shifted(axes, d)])


def give(v, axes, d):
    return lax.ppermute(v, ALL, shifted(axes, d))


def ring(v, axes):
    return [v] + [fetch(v, axes, d) for d in range(1, 4)]


def gathered_sum(v, axes):
    p = ring(v, axes)
    return (p[0] + p[2]) + (p[1] + p[3])


def returned(vs, axes):
    return [vs[0]] + [give(vs[d], axes, d) for d in range(1, len(vs))]


def steps(target_xyz, source_xyz, target_count, source_count, psi, omega):
    z, x, core, yq = (lax.axis_index(n) for n in ALL)
    along = jnp.where(core == 0, x, z)
    across = jnp.where(core == 0, z, x)
    where = jnp.stack([yq, target_count[0], source_count[0], core, along, across])
    where = where.astype(jnp.int32)
    tpay, spay = pack(where, target_xyz, source_xyz, psi, omega)
    trow = ring(tpay, FIRST)
    srow = ring(spay, SAME["y"])
    column = jnp.stack(trow)
    tin = [column]
    for d in (1, 2, 3):
        tin.append(fetch(column, LAST, d))
    srep = jnp.stack(srow)
    sfar = fetch(srep, SAME["c"], 1)
    src = sources([srep, sfar])
    y0, za = sketch(tin[0:1], src)
    y1, y2, zb = sketch(tin[1:3], src)
    y3, z0, z1 = sketch(tin[3:4], src, (za, zb))
    ys = [y0, y1, y2, y3]
    zfar = give(z1, SAME["c"], 1)
    ys[1:3] = [give(ys[d], LAST, d) for d in (1, 2)]
    ys[3] = give(ys[3], LAST, 3)
    zmine = [z0[d] + zfar[d] for d in range(YN)]
    zs = returned(zmine, SAME["y"])
    ys = [(ys[0][d] + ys[1][d]) + (ys[2][d] + ys[3][d]) for d in range(ZN)]
    ys = returned(ys, FIRST)
    yfin, zfin, keep, send = finish(where, ys, zs, tpay)
    ys = ring(yfin, SAME["y"])
    half = keep + fetch(send, SAME["c"], 1)
    half = half.reshape(3, ZN, R // CN // ZN, R)
    chunks = [
        lax.dynamic_index_in_dim(half, lax.rem(along + d, ZN), 1, keepdims=False)
        for d in range(ZN)
    ]
    p = returned(chunks, FIRST)
    mine = (p[0] + p[1]) + (p[2] + p[3])
    mine = gathered_sum(gathered_sum(mine, LAST), SAME["y"])
    own = ring(mine, FIRST)
    other = fetch(jnp.stack(own), SAME["c"], 1)
    y, g0, g1, g2 = place(where, ys, own, other)
    return (y, zfin, g0, g1, g2)


def solution(mesh):
    grid = Mesh(mesh.devices.reshape(ZN, XN, CN, YN), ALL)
    pts = ("z", "x", "c")
    return jax.shard_map(
        steps,
        mesh=grid,
        in_specs=(P(None, pts), P(None, ALL), P(pts), P(ALL), P(pts, None), P(ALL, None)),
        out_specs=(P(pts, None), P(ALL, None), P(), P(), P()),
        check_vma=False,
    )
```

```python
import functools
import math

import jax
import jax.numpy as jnp
from jax import lax
from jax.experimental import pallas as pl
from jax.experimental.pallas import tpu as pltpu
from jax.sharding import Mesh, PartitionSpec as P


SHIFT = 1.05
SPREAD = 8.0
ZN, XN, CN, YN = 4, 4, 2, 4
ALL = ("z", "x", "c", "y")
R = 256
TCAP, SCAP = 1024, 512
TQ = TCAP // YN
GRAN = 16
NT = ZN * XN
NS = CN * YN
TC = 256
SC = 512
TPAY = TQ + 32
SPAY = SCAP + 64
FAR = 4.0
F32 = jnp.float32
BF16 = jnp.bfloat16


def inside(*arrays):
    return [pltpu.with_memory_space_constraint(v, pltpu.VMEM) for v in arrays]


def three_pieces(v):
    hi = v.astype(BF16)
    rest = v - hi.astype(F32)
    mid = rest.astype(BF16)
    low = (rest - mid.astype(F32)).astype(BF16)
    return hi, mid, low


def pack_kernel(where_ref, txyz_ref, sxyz_ref, psi_ref, omega_ref, tpay_ref, spay_ref, cols, quarter):
    yq = where_ref[0]
    tcount = where_ref[1]
    scount = where_ref[2]
    rows16 = lax.broadcasted_iota(jnp.int32, (GRAN, R), 0)
    cols[...] = jnp.concatenate(
        [txyz_ref[...], jnp.zeros((5, TCAP), F32)], axis=0
    ).T
    for a in range(TQ // GRAN):
        start = pl.multiple_of((a * YN + yq) * GRAN, GRAN)
        block = psi_ref[pl.ds(start, GRAN), :]
        tpay_ref[a * GRAN:(a + 1) * GRAN, :] = jnp.where(
            rows16 + start < tcount, block, jnp.zeros_like(block)
        )
        quarter[a * GRAN:(a + 1) * GRAN, :] = cols[pl.ds(start, GRAN), :]
    step = GRAN * YN
    tlive = (tcount // step) * GRAN + jnp.clip(tcount % step - yq * GRAN, 0, GRAN)
    sub = lax.broadcasted_iota(jnp.int32, (8, TQ), 0)
    tpos = quarter[...].T
    tpos = jnp.where((sub == 1) | (sub == 2), tpos * SPREAD, tpos)
    tpos = jnp.where(sub == 3, tlive.astype(F32), tpos)
    tail = jnp.zeros((8, R), BF16)
    tpay_ref[TQ:TPAY, :] = jnp.concatenate([*three_pieces(tpos), tail], axis=0)
    srow = lax.broadcasted_iota(jnp.int32, (SCAP, R), 0)
    om = omega_ref[...]
    spay_ref[0:SCAP, :] = jnp.where(srow < scount, om, jnp.zeros_like(om))
    for h in range(SCAP // R):
        part = jnp.concatenate(
            [sxyz_ref[:, h * R:(h + 1) * R], jnp.zeros((5, R), F32)], axis=0
        )
        part = jnp.where((sub == 1) | (sub == 2), part * SPREAD, part)
        part = jnp.where(sub == 0, part + SHIFT, part)
        part = jnp.where(sub == 3, (scount - h * R).clip(0, R).astype(F32), part)
        base = SCAP + 32 * h
        spay_ref[base:base + 32, :] = jnp.concatenate([*three_pieces(part), tail], axis=0)


def pack(where, txyz, sxyz, psi, omega):
    vm = pl.BlockSpec(memory_space=pltpu.VMEM)
    return pl.pallas_call(
        pack_kernel,
        out_shape=(
            jax.ShapeDtypeStruct((TPAY, R), BF16),
            jax.ShapeDtypeStruct((SPAY, R), BF16),
        ),
        in_specs=[pl.BlockSpec(memory_space=pltpu.SMEM), vm, vm, vm, vm],
        out_specs=(vm, vm),
        scratch_shapes=[pltpu.VMEM((TCAP, 8), F32), pltpu.VMEM((TQ, 8), F32)],
    )(where, txyz, sxyz, psi, omega)


def join(ref, *at):
    lo = at[-1]
    lead = at[:-1]
    v = ref[(*lead, slice(lo, lo + 32), slice(None))].astype(F32)
    return v[0:8] + v[8:16] + v[16:24]


def ceil16(n):
    return ((n + GRAN - 1) // GRAN) * GRAN


TROWS = 2 * TC
SROWS = NS * SCAP + 2 * SC


def first_lane(row):
    return jnp.max(row).astype(jnp.int32)


def offsets(counts):
    off = [jnp.int32(0)]
    for n in counts:
        off.append(off[-1] + ceil16(n))
    return [pl.multiple_of(v, GRAN) for v in off]


def sources_kernel(s0, s1, omc, srow, scnt, spos):
    sin = (s0, s1)
    counts = []
    for k in range(NS):
        both = [join(sin[k // YN], k % YN, SCAP + 32 * h)[3:4, 0:128] for h in range(SCAP // R)]
        scnt[k:k + 1, :] = sum(both)
        counts.append(first_lane(sum(both)))
    soff = offsets(counts)
    chunks = (soff[NS] + SC - 1) // SC
    scnt[NS:NS + 1, :] = jnp.full((1, 128), chunks.astype(F32))
    for k in range(NS):
        ref, d = sin[k // YN], k % YN
        omc[pl.ds(soff[k], SCAP), :] = ref[d, 0:SCAP, :]
        for h in range(SCAP // R):
            spos[pl.ds(soff[k] + h * R, R), :] = join(ref, d, SCAP + 32 * h).T
    omc[pl.ds(soff[NS], SC), :] = jnp.zeros((SC, R), BF16)
    spos[pl.ds(soff[NS], SC), :] = jnp.full((SC, 8), FAR, F32)

    def prepare(si, carry):
        srow[si] = spos[pl.ds(pl.multiple_of(si * SC, SC), SC), :].T
        return carry

    lax.fori_loop(0, chunks, prepare, 0)


def sources(sin):
    vm = pl.BlockSpec(memory_space=pltpu.VMEM)
    return pl.pallas_call(
        sources_kernel,
        out_shape=(
            jax.ShapeDtypeStruct((SROWS, R), BF16),
            jax.ShapeDtypeStruct((SROWS // SC, 8, SC), F32),
            jax.ShapeDtypeStruct((2 * NS, 128), F32),
        ),
        in_specs=[vm] * 2,
        out_specs=(vm,) * 3,
        scratch_shapes=[
            pltpu.VMEM((SROWS, 8), F32),
        ],
        compiler_params=pltpu.CompilerParams(vmem_limit_bytes=5 << 20),
    )(*inside(*sin))


def sketch_kernel(m, last, *refs):
    groups = m * ZN
    tin, refs = refs[:m], refs[m:]
    omc, srow, scnt = refs[:3]
    refs = refs[3:]
    if last:
        earlier, refs = refs[:3], refs[3:]
    youts, refs = refs[:m], refs[m:]
    if last:
        zouts, refs = refs[:2], refs[2:]
        psic, tpos, bcx, bcy, bcz, yc, tile0, tile1, zc = refs
    else:
        zc, psic, tpos, bcx, bcy, bcz, yc, tile0, tile1 = refs
    ns = first_lane(scnt[NS:NS + 1, :])
    toff = offsets(
        [first_lane(join(tin[k // ZN], k % ZN, TQ)[3:4, 0:128]) for k in range(groups)]
    )
    for k in range(groups):
        ref, d = tin[k // ZN], k % ZN
        psic[pl.ds(toff[k], TQ), :] = ref[d, 0:TQ, :]
        tpos[pl.ds(toff[k], TQ), :] = join(ref, d, TQ).T
    psic[pl.ds(toff[groups], 2 * TC), :] = jnp.zeros((2 * TC, R), BF16)
    tpos[pl.ds(toff[groups], 2 * TC), :] = jnp.zeros((2 * TC, 8), F32)
    nt = (toff[groups] + TC - 1) // TC

    def clear(si, carry):
        zc[pl.ds(pl.multiple_of(si * SC, SC), SC), :] = jnp.zeros((SC, R), F32)
        return carry

    lax.fori_loop(0, ns, clear, 0)

    def columns(ti, carry):
        ta = pl.multiple_of(ti * TC, TC)
        tp = tpos[pl.ds(ta, TC), :]
        bcx[ti] = jnp.broadcast_to(tp[:, 0:1], (TC, 128))
        bcy[ti] = jnp.broadcast_to(tp[:, 1:2], (TC, 128))
        bcz[ti] = jnp.broadcast_to(tp[:, 2:3], (TC, 128))
        yc[pl.ds(ta, TC), :] = jnp.zeros((TC, R), F32)
        return carry

    lax.fori_loop(0, nt + 1, columns, 0)

    def make(at, tile):
        ti, si = at
        for j in range(SC // 128):
            lanes = slice(j * 128, (j + 1) * 128)
            dx = bcx[ti] - srow[si, 0:1, lanes]
            dy = bcy[ti] - srow[si, 1:2, lanes]
            dz = bcz[ti] - srow[si, 2:3, lanes]
            tile[:, lanes] = lax.rsqrt(dx * dx + dy * dy + dz * dz).astype(BF16)

    def use(at, tile):
        ta = pl.multiple_of(at[0] * TC, TC)
        sa = pl.multiple_of(at[1] * SC, SC)
        block = tile[...]
        yc[pl.ds(ta, TC), :] += jnp.dot(
            block, omc[pl.ds(sa, SC), :], preferred_element_type=F32
        )
        zc[pl.ds(sa, SC), :] += lax.dot_general(
            block, psic[pl.ds(ta, TC), :], (((0,), (0,)), ((), ())),
            preferred_element_type=F32,
        )

    def after(at):
        wrap = at[1] + 1 == ns
        return jnp.where(wrap, at[0] + 1, at[0]), jnp.where(wrap, 0, at[1] + 1)

    start = (jnp.int32(0), jnp.int32(0))
    make(start, tile0)

    def two_steps(p, first):
        second = after(first)
        use(first, tile0)
        make(second, tile1)
        third = after(second)
        use(second, tile1)
        make(third, tile0)
        return third

    lax.fori_loop(0, (nt * ns + 1) // 2, two_steps, start)
    for k in range(groups):
        youts[k // ZN][k % ZN] = yc[pl.ds(toff[k], TQ), :]
    if last:
        soff = offsets([first_lane(scnt[k:k + 1, :]) for k in range(NS)])
        for k in range(NS):
            rows = pl.ds(soff[k], SCAP)
            total = zc[rows, :] + earlier[2][rows, :]
            total = total + (earlier[0][rows, :] + earlier[1][rows, :])
            zouts[k // YN][k % YN] = total


def sketch(tin, src, earlier=None):
    m = len(tin)
    last = earlier is not None
    vm = pl.BlockSpec(memory_space=pltpu.VMEM)
    trows = m * ZN * TQ + TROWS
    ypart = jax.ShapeDtypeStruct((ZN, TQ, R), F32)
    zhalf = jax.ShapeDtypeStruct((YN, SCAP, R), F32)
    zall = (SROWS, R)
    outs = [ypart] * m + ([zhalf] * CN if last else [jax.ShapeDtypeStruct(zall, F32)])
    operands = [*tin, *src, *(earlier or ())]
    column = pltpu.VMEM((trows // TC, TC, 128), F32)
    scratch = [
        pltpu.VMEM((trows, R), BF16),
        pltpu.VMEM((trows, 8), F32),
        column,
        column,
        column,
        pltpu.VMEM((trows, R), F32),
        pltpu.VMEM((TC, SC), BF16),
        pltpu.VMEM((TC, SC), BF16),
    ]
    return pl.pallas_call(
        functools.partial(sketch_kernel, m, last),
        out_shape=tuple(outs),
        in_specs=[vm] * len(operands),
        out_specs=(vm,) * len(outs),
        scratch_shapes=scratch + ([pltpu.VMEM(zall, F32)] if last else []),
        compiler_params=pltpu.CompilerParams(vmem_limit_bytes=(8 + 5 * m + 6 * last) << 20),
    )(*inside(*operands))


def finish_kernel(where_ref, y0, y1, y2, y3, z0, z1, z2, z3, tpay,
                  yfin_ref, zfin_ref, keep_ref, send_ref, *, yscale, zscale, tn, sn):
    yq, tcount, scount, core = where_ref[0], where_ref[1], where_ref[2], where_ref[3]
    q = lax.broadcasted_iota(jnp.int32, (TQ, R), 0)
    slot = (q // GRAN) * (GRAN * YN) + yq * GRAN + q % GRAN
    total = (y0[...] + y1[...]) + (y2[...] + y3[...])
    yfin_ref[...] = jnp.where(slot < tcount, total * yscale, 0.0)
    srow = lax.broadcasted_iota(jnp.int32, (SCAP, R), 0)
    total = (z0[...] + z1[...]) + (z2[...] + z3[...])
    zfin_ref[...] = jnp.where(srow < scount, total * zscale, 0.0)
    psi = tpay[0:TQ, :].astype(F32)
    y, z = yfin_ref[...], zfin_ref[...]
    hi = lax.Precision.HIGHEST
    dims = (((0,), (0,)), ((), ()))
    parts = (
        lax.dot_general(psi, y, dims, precision=hi, preferred_element_type=F32) / math.sqrt(tn),
        lax.dot_general(y, y, dims, precision=hi, preferred_element_type=F32) / tn,
        lax.dot_general(z, z, dims, precision=hi, preferred_element_type=F32) / sn,
    )
    first = core == 0
    for k in range(3):
        top, low = parts[k][0:R // 2, :], parts[k][R // 2:, :]
        keep_ref[k] = jnp.where(first, top, low)
        send_ref[k] = jnp.where(first, low, top)


def finish(where, y, z, tpay):
    tn, sn = TCAP * NT * CN, SCAP * NT * NS
    vm = pl.BlockSpec(memory_space=pltpu.VMEM)
    half = jax.ShapeDtypeStruct((3, R // 2, R), F32)

    def body(*refs):
        finish_kernel(
            *refs, yscale=2.0 / math.sqrt(sn), zscale=2.0 / math.sqrt(tn), tn=tn, sn=sn
        )

    return pl.pallas_call(
        body,
        out_shape=(
            jax.ShapeDtypeStruct((TQ, R), F32),
            jax.ShapeDtypeStruct((SCAP, R), F32),
            half,
            half,
        ),
        in_specs=[pl.BlockSpec(memory_space=pltpu.SMEM)] + [vm] * 9,
        out_specs=(vm,) * 4,
        compiler_params=pltpu.CompilerParams(vmem_limit_bytes=14 << 20),
    )(where, *inside(*y, *z, tpay))


def place_kernel(where_ref, *refs):
    ys, own, other = refs[0:YN], refs[YN:YN + ZN], refs[YN + ZN]
    yout, outs = refs[YN + ZN + 1], refs[YN + ZN + 2:]
    yq, core = where_ref[0], where_ref[3]
    for d in range(YN):
        q = lax.rem(yq + d, YN)
        for a in range(TQ // GRAN):
            at = pl.multiple_of((a * YN + q) * GRAN, GRAN)
            yout[pl.ds(at, GRAN), :] = ys[d][a * GRAN:(a + 1) * GRAN, :]
    share = R // CN // ZN
    for d in range(ZN):
        q = lax.rem(where_ref[4] + d, ZN)
        at = pl.multiple_of((core * ZN + q) * share, share)
        q = lax.rem(where_ref[5] + d, ZN)
        far = pl.multiple_of(((1 - core) * ZN + q) * share, share)
        for k in range(3):
            outs[k][pl.ds(at, share), :] = own[d][k]
            outs[k][pl.ds(far, share), :] = other[d, k]


def place(where, ys, own, other):
    vm = pl.BlockSpec(memory_space=pltpu.VMEM)
    return pl.pallas_call(
        place_kernel,
        out_shape=(
            jax.ShapeDtypeStruct((TCAP, R), F32),
            *[jax.ShapeDtypeStruct((R, R), F32)] * 3,
        ),
        in_specs=[pl.BlockSpec(memory_space=pltpu.SMEM)] + [vm] * (YN + ZN + 1),
        out_specs=(vm,) * 4,
        compiler_params=pltpu.CompilerParams(vmem_limit_bytes=10 << 20),
    )(where, *inside(*ys, *own, other))


FIRST = ("x", "z")
LAST = ("z", "x")
SAME = {name: (name, name) for name in ALL}


def shifted(axes, d):
    pairs = []
    size = dict(z=ZN, x=XN, c=CN, y=YN)
    for z in range(ZN):
        for x in range(XN):
            for c in range(CN):
                for y in range(YN):
                    at = dict(z=z, x=x, c=c, y=y)
                    to = dict(at)
                    to[axes[c]] = (at[axes[c]] + d) % size[axes[c]]
                    flat = [((p["z"] * XN + p["x"]) * CN + p["c"]) * YN + p["y"] for p in (at, to)]
                    pairs.append(tuple(flat))
    return pairs


def fetch(v, axes, d):
    return lax.ppermute(v, ALL, [(b, a) for a, b in shifted(axes, d)])


def give(v, axes, d):
    return lax.ppermute(v, ALL, shifted(axes, d))


def ring(v, axes):
    return [v] + [fetch(v, axes, d) for d in range(1, 4)]


def gathered_sum(v, axes):
    p = ring(v, axes)
    return (p[0] + p[2]) + (p[1] + p[3])


def returned(vs, axes):
    return [vs[0]] + [give(vs[d], axes, d) for d in range(1, len(vs))]


def steps(target_xyz, source_xyz, target_count, source_count, psi, omega):
    z, x, core, yq = (lax.axis_index(n) for n in ALL)
    along = jnp.where(core == 0, x, z)
    across = jnp.where(core == 0, z, x)
    where = jnp.stack([yq, target_count[0], source_count[0], core, along, across])
    where = where.astype(jnp.int32)
    tpay, spay = pack(where, target_xyz, source_xyz, psi, omega)
    trow = ring(tpay, FIRST)
    srow = ring(spay, SAME["y"])
    column = jnp.stack(trow)
    tin = [column]
    for d in (1, 2, 3):
        tin.append(fetch(column, LAST, d))
    srep = jnp.stack(srow)
    sfar = fetch(srep, SAME["c"], 1)
    src = sources([srep, sfar])
    y0, za = sketch(tin[0:1], src)
    y1, zb = sketch(tin[1:2], src)
    y3, zd = sketch(tin[3:4], src)
    y2, z0, z1 = sketch(tin[2:3], src, (za, zb, zd))
    ys = [y0, y1, y2, y3]
    zfar = give(z1, SAME["c"], 1)
    ys[1] = give(ys[1], LAST, 1)
    ys[3] = give(ys[3], LAST, 3)
    ys[2] = give(ys[2], LAST, 2)
    zmine = [z0[d] + zfar[d] for d in range(YN)]
    zs = returned(zmine, SAME["y"])
    ys = [(ys[0][d] + ys[1][d]) + (ys[2][d] + ys[3][d]) for d in range(ZN)]
    ys = returned(ys, FIRST)
    yfin, zfin, keep, send = finish(where, ys, zs, tpay)
    ys = ring(yfin, SAME["y"])
    half = keep + fetch(send, SAME["c"], 1)
    half = half.reshape(3, ZN, R // CN // ZN, R)
    chunks = [
        lax.dynamic_index_in_dim(half, lax.rem(along + d, ZN), 1, keepdims=False)
        for d in range(ZN)
    ]
    p = returned(chunks, FIRST)
    mine = (p[0] + p[1]) + (p[2] + p[3])
    mine = gathered_sum(gathered_sum(mine, LAST), SAME["y"])
    own = ring(mine, FIRST)
    other = fetch(jnp.stack(own), SAME["c"], 1)
    y, g0, g1, g2 = place(where, ys, own, other)
    return (y, zfin, g0, g1, g2)


def solution(mesh):
    grid = Mesh(mesh.devices.reshape(ZN, XN, CN, YN), ALL)
    pts = ("z", "x", "c")
    return jax.shard_map(
        steps,
        mesh=grid,
        in_specs=(P(None, pts), P(None, ALL), P(pts), P(ALL), P(pts, None), P(ALL, None)),
        out_specs=(P(pts, None), P(ALL, None), P(), P(), P()),
        check_vma=False,
    )
```

```python
import functools
import math

import jax
import jax.numpy as jnp
from jax import lax
from jax.experimental import pallas as pl
from jax.experimental.pallas import tpu as pltpu
from jax.sharding import Mesh, PartitionSpec as P


SHIFT = 1.05
SPREAD = 8.0
ZN, XN, CN, YN = 4, 4, 2, 4
ALL = ("z", "x", "c", "y")
R = 256
TCAP, SCAP = 1024, 512
TQ = TCAP // YN
GRAN = 16
NT = ZN * XN
NS = CN * YN
TC = 256
SC = 512
TPAY = TQ + 32
SPAY = SCAP + 64
FAR = 4.0
F32 = jnp.float32
BF16 = jnp.bfloat16


def inside(*arrays):
    return [pltpu.with_memory_space_constraint(v, pltpu.VMEM) for v in arrays]


def three_pieces(v):
    hi = v.astype(BF16)
    rest = v - hi.astype(F32)
    mid = rest.astype(BF16)
    low = (rest - mid.astype(F32)).astype(BF16)
    return hi, mid, low


def pack_kernel(where_ref, txyz_ref, sxyz_ref, psi_ref, omega_ref, tpay_ref, spay_ref, cols, quarter):
    yq = where_ref[0]
    tcount = where_ref[1]
    scount = where_ref[2]
    rows16 = lax.broadcasted_iota(jnp.int32, (GRAN, R), 0)
    cols[...] = jnp.concatenate(
        [txyz_ref[...], jnp.zeros((5, TCAP), F32)], axis=0
    ).T
    for a in range(TQ // GRAN):
        start = pl.multiple_of((a * YN + yq) * GRAN, GRAN)
        block = psi_ref[pl.ds(start, GRAN), :]
        tpay_ref[a * GRAN:(a + 1) * GRAN, :] = jnp.where(
            rows16 + start < tcount, block, jnp.zeros_like(block)
        )
        quarter[a * GRAN:(a + 1) * GRAN, :] = cols[pl.ds(start, GRAN), :]
    step = GRAN * YN
    tlive = (tcount // step) * GRAN + jnp.clip(tcount % step - yq * GRAN, 0, GRAN)
    sub = lax.broadcasted_iota(jnp.int32, (8, TQ), 0)
    tpos = quarter[...].T
    tpos = jnp.where((sub == 1) | (sub == 2), tpos * SPREAD, tpos)
    tpos = jnp.where(sub == 3, tlive.astype(F32), tpos)
    tail = jnp.zeros((8, R), BF16)
    tpay_ref[TQ:TPAY, :] = jnp.concatenate([*three_pieces(tpos), tail], axis=0)
    srow = lax.broadcasted_iota(jnp.int32, (SCAP, R), 0)
    om = omega_ref[...]
    spay_ref[0:SCAP, :] = jnp.where(srow < scount, om, jnp.zeros_like(om))
    for h in range(SCAP // R):
        part = jnp.concatenate(
            [sxyz_ref[:, h * R:(h + 1) * R], jnp.zeros((5, R), F32)], axis=0
        )
        part = jnp.where((sub == 1) | (sub == 2), part * SPREAD, part)
        part = jnp.where(sub == 0, part + SHIFT, part)
        part = jnp.where(sub == 3, (scount - h * R).clip(0, R).astype(F32), part)
        base = SCAP + 32 * h
        spay_ref[base:base + 32, :] = jnp.concatenate([*three_pieces(part), tail], axis=0)


def pack(where, txyz, sxyz, psi, omega):
    vm = pl.BlockSpec(memory_space=pltpu.VMEM)
    return pl.pallas_call(
        pack_kernel,
        out_shape=(
            jax.ShapeDtypeStruct((TPAY, R), BF16),
            jax.ShapeDtypeStruct((SPAY, R), BF16),
        ),
        in_specs=[pl.BlockSpec(memory_space=pltpu.SMEM), vm, vm, vm, vm],
        out_specs=(vm, vm),
        scratch_shapes=[pltpu.VMEM((TCAP, 8), F32), pltpu.VMEM((TQ, 8), F32)],
    )(where, txyz, sxyz, psi, omega)


def join(ref, *at):
    lo = at[-1]
    lead = at[:-1]
    v = ref[(*lead, slice(lo, lo + 32), slice(None))].astype(F32)
    return v[0:8] + v[8:16] + v[16:24]


def ceil16(n):
    return ((n + GRAN - 1) // GRAN) * GRAN


TROWS = 2 * TC
SROWS = NS * SCAP + 2 * SC


def first_lane(row):
    return jnp.max(row).astype(jnp.int32)


def offsets(counts):
    off = [jnp.int32(0)]
    for n in counts:
        off.append(off[-1] + ceil16(n))
    return [pl.multiple_of(v, GRAN) for v in off]


def sources_kernel(*refs):
    sin, (omc, srow, scnt, spos) = refs[:NS], refs[NS:]
    counts = []
    for k in range(NS):
        both = [join(sin[k], SCAP + 32 * h)[3:4, 0:128] for h in range(SCAP // R)]
        scnt[k:k + 1, :] = sum(both)
        counts.append(first_lane(sum(both)))
    soff = offsets(counts)
    chunks = (soff[NS] + SC - 1) // SC
    scnt[NS:NS + 1, :] = jnp.full((1, 128), chunks.astype(F32))
    for k in range(NS):
        omc[pl.ds(soff[k], SCAP), :] = sin[k][0:SCAP, :]
        for h in range(SCAP // R):
            spos[pl.ds(soff[k] + h * R, R), :] = join(sin[k], SCAP + 32 * h).T
    omc[pl.ds(soff[NS], SC), :] = jnp.zeros((SC, R), BF16)
    spos[pl.ds(soff[NS], SC), :] = jnp.full((SC, 8), FAR, F32)

    def prepare(si, carry):
        srow[si] = spos[pl.ds(pl.multiple_of(si * SC, SC), SC), :].T
        return carry

    lax.fori_loop(0, chunks, prepare, 0)


def sources(sin):
    vm = pl.BlockSpec(memory_space=pltpu.VMEM)
    return pl.pallas_call(
        sources_kernel,
        out_shape=(
            jax.ShapeDtypeStruct((SROWS, R), BF16),
            jax.ShapeDtypeStruct((SROWS // SC, 8, SC), F32),
            jax.ShapeDtypeStruct((2 * NS, 128), F32),
        ),
        in_specs=[vm] * NS,
        out_specs=(vm,) * 3,
        scratch_shapes=[
            pltpu.VMEM((SROWS, 8), F32),
        ],
        compiler_params=pltpu.CompilerParams(vmem_limit_bytes=5 << 20),
    )(*inside(*sin))


def sketch_kernel(m, last, *refs):
    groups = m * ZN
    tin, refs = refs[:m], refs[m:]
    omc, srow, scnt = refs[:3]
    refs = refs[3:]
    if last:
        earlier, refs = refs[:3], refs[3:]
    youts, refs = refs[:m], refs[m:]
    if last:
        zouts, refs = refs[:2], refs[2:]
        psic, tpos, bcx, bcy, bcz, yc, tile0, tile1, zc = refs
    else:
        zc, psic, tpos, bcx, bcy, bcz, yc, tile0, tile1 = refs
    ns = first_lane(scnt[NS:NS + 1, :])
    toff = offsets(
        [first_lane(join(tin[k // ZN], k % ZN, TQ)[3:4, 0:128]) for k in range(groups)]
    )
    for k in range(groups):
        ref, d = tin[k // ZN], k % ZN
        psic[pl.ds(toff[k], TQ), :] = ref[d, 0:TQ, :]
        tpos[pl.ds(toff[k], TQ), :] = join(ref, d, TQ).T
    psic[pl.ds(toff[groups], 2 * TC), :] = jnp.zeros((2 * TC, R), BF16)
    tpos[pl.ds(toff[groups], 2 * TC), :] = jnp.zeros((2 * TC, 8), F32)
    nt = (toff[groups] + TC - 1) // TC

    def clear(si, carry):
        zc[pl.ds(pl.multiple_of(si * SC, SC), SC), :] = jnp.zeros((SC, R), F32)
        return carry

    lax.fori_loop(0, ns, clear, 0)

    def columns(ti, carry):
        ta = pl.multiple_of(ti * TC, TC)
        tp = tpos[pl.ds(ta, TC), :]
        bcx[ti] = jnp.broadcast_to(tp[:, 0:1], (TC, 128))
        bcy[ti] = jnp.broadcast_to(tp[:, 1:2], (TC, 128))
        bcz[ti] = jnp.broadcast_to(tp[:, 2:3], (TC, 128))
        yc[pl.ds(ta, TC), :] = jnp.zeros((TC, R), F32)
        return carry

    lax.fori_loop(0, nt + 1, columns, 0)

    def make(at, tile):
        ti, si = at
        for j in range(SC // 128):
            lanes = slice(j * 128, (j + 1) * 128)
            dx = bcx[ti] - srow[si, 0:1, lanes]
            dy = bcy[ti] - srow[si, 1:2, lanes]
            dz = bcz[ti] - srow[si, 2:3, lanes]
            tile[:, lanes] = lax.rsqrt(dx * dx + dy * dy + dz * dz).astype(BF16)

    def use(at, tile):
        ta = pl.multiple_of(at[0] * TC, TC)
        sa = pl.multiple_of(at[1] * SC, SC)
        block = tile[...]
        yc[pl.ds(ta, TC), :] += jnp.dot(
            block, omc[pl.ds(sa, SC), :], preferred_element_type=F32
        )
        zc[pl.ds(sa, SC), :] += lax.dot_general(
            block, psic[pl.ds(ta, TC), :], (((0,), (0,)), ((), ())),
            preferred_element_type=F32,
        )

    def after(at):
        wrap = at[1] + 1 == ns
        return jnp.where(wrap, at[0] + 1, at[0]), jnp.where(wrap, 0, at[1] + 1)

    start = (jnp.int32(0), jnp.int32(0))
    make(start, tile0)

    def two_steps(p, first):
        second = after(first)
        use(first, tile0)
        make(second, tile1)
        third = after(second)
        use(second, tile1)
        make(third, tile0)
        return third

    lax.fori_loop(0, (nt * ns + 1) // 2, two_steps, start)
    for k in range(groups):
        youts[k // ZN][k % ZN] = yc[pl.ds(toff[k], TQ), :]
    if last:
        soff = offsets([first_lane(scnt[k:k + 1, :]) for k in range(NS)])
        for k in range(NS):
            rows = pl.ds(soff[k], SCAP)
            total = zc[rows, :] + earlier[2][rows, :]
            total = total + (earlier[0][rows, :] + earlier[1][rows, :])
            zouts[k // YN][k % YN] = total


def sketch(tin, src, earlier=None):
    m = len(tin)
    last = earlier is not None
    vm = pl.BlockSpec(memory_space=pltpu.VMEM)
    trows = m * ZN * TQ + TROWS
    ypart = jax.ShapeDtypeStruct((ZN, TQ, R), F32)
    zhalf = jax.ShapeDtypeStruct((YN, SCAP, R), F32)
    zall = (SROWS, R)
    outs = [ypart] * m + ([zhalf] * CN if last else [jax.ShapeDtypeStruct(zall, F32)])
    operands = [*tin, *src, *(earlier or ())]
    column = pltpu.VMEM((trows // TC, TC, 128), F32)
    scratch = [
        pltpu.VMEM((trows, R), BF16),
        pltpu.VMEM((trows, 8), F32),
        column,
        column,
        column,
        pltpu.VMEM((trows, R), F32),
        pltpu.VMEM((TC, SC), BF16),
        pltpu.VMEM((TC, SC), BF16),
    ]
    return pl.pallas_call(
        functools.partial(sketch_kernel, m, last),
        out_shape=tuple(outs),
        in_specs=[vm] * len(operands),
        out_specs=(vm,) * len(outs),
        scratch_shapes=scratch + ([pltpu.VMEM(zall, F32)] if last else []),
        compiler_params=pltpu.CompilerParams(vmem_limit_bytes=(8 + 5 * m + 6 * last) << 20),
    )(*inside(*operands))


def finish_kernel(where_ref, y0, y1, y2, y3, z0, z1, z2, z3, tpay,
                  yfin_ref, zfin_ref, keep_ref, send_ref, *, yscale, zscale, tn, sn):
    yq, tcount, scount, core = where_ref[0], where_ref[1], where_ref[2], where_ref[3]
    q = lax.broadcasted_iota(jnp.int32, (TQ, R), 0)
    slot = (q // GRAN) * (GRAN * YN) + yq * GRAN + q % GRAN
    total = (y0[...] + y1[...]) + (y2[...] + y3[...])
    yfin_ref[...] = jnp.where(slot < tcount, total * yscale, 0.0)
    srow = lax.broadcasted_iota(jnp.int32, (SCAP, R), 0)
    total = (z0[...] + z1[...]) + (z2[...] + z3[...])
    zfin_ref[...] = jnp.where(srow < scount, total * zscale, 0.0)
    psi = tpay[0:TQ, :].astype(F32)
    y, z = yfin_ref[...], zfin_ref[...]
    hi = lax.Precision.HIGHEST
    dims = (((0,), (0,)), ((), ()))
    parts = (
        lax.dot_general(psi, y, dims, precision=hi, preferred_element_type=F32) / math.sqrt(tn),
        lax.dot_general(y, y, dims, precision=hi, preferred_element_type=F32) / tn,
        lax.dot_general(z, z, dims, precision=hi, preferred_element_type=F32) / sn,
    )
    first = core == 0
    for k in range(3):
        top, low = parts[k][0:R // 2, :], parts[k][R // 2:, :]
        keep_ref[k] = jnp.where(first, top, low)
        send_ref[k] = jnp.where(first, low, top)


def finish(where, y, z, tpay):
    tn, sn = TCAP * NT * CN, SCAP * NT * NS
    vm = pl.BlockSpec(memory_space=pltpu.VMEM)
    half = jax.ShapeDtypeStruct((3, R // 2, R), F32)

    def body(*refs):
        finish_kernel(
            *refs, yscale=2.0 / math.sqrt(sn), zscale=2.0 / math.sqrt(tn), tn=tn, sn=sn
        )

    return pl.pallas_call(
        body,
        out_shape=(
            jax.ShapeDtypeStruct((TQ, R), F32),
            jax.ShapeDtypeStruct((SCAP, R), F32),
            half,
            half,
        ),
        in_specs=[pl.BlockSpec(memory_space=pltpu.SMEM)] + [vm] * 9,
        out_specs=(vm,) * 4,
        compiler_params=pltpu.CompilerParams(vmem_limit_bytes=14 << 20),
    )(where, *inside(*y, *z, tpay))


def place_kernel(where_ref, *refs):
    ys, own, other = refs[0:YN], refs[YN:YN + ZN], refs[YN + ZN]
    yout, outs = refs[YN + ZN + 1], refs[YN + ZN + 2:]
    yq, core = where_ref[0], where_ref[3]
    for d in range(YN):
        q = lax.rem(yq + d, YN)
        for a in range(TQ // GRAN):
            at = pl.multiple_of((a * YN + q) * GRAN, GRAN)
            yout[pl.ds(at, GRAN), :] = ys[d][a * GRAN:(a + 1) * GRAN, :]
    share = R // CN // ZN
    for d in range(ZN):
        q = lax.rem(where_ref[4] + d, ZN)
        at = pl.multiple_of((core * ZN + q) * share, share)
        q = lax.rem(where_ref[5] + d, ZN)
        far = pl.multiple_of(((1 - core) * ZN + q) * share, share)
        for k in range(3):
            outs[k][pl.ds(at, share), :] = own[d][k]
            outs[k][pl.ds(far, share), :] = other[d, k]


def place(where, ys, own, other):
    vm = pl.BlockSpec(memory_space=pltpu.VMEM)
    return pl.pallas_call(
        place_kernel,
        out_shape=(
            jax.ShapeDtypeStruct((TCAP, R), F32),
            *[jax.ShapeDtypeStruct((R, R), F32)] * 3,
        ),
        in_specs=[pl.BlockSpec(memory_space=pltpu.SMEM)] + [vm] * (YN + ZN + 1),
        out_specs=(vm,) * 4,
        compiler_params=pltpu.CompilerParams(vmem_limit_bytes=10 << 20),
    )(where, *inside(*ys, *own, other))


FIRST = ("x", "z")
LAST = ("z", "x")
SAME = {name: (name, name) for name in ALL}


def shifted(axes, d):
    pairs = []
    size = dict(z=ZN, x=XN, c=CN, y=YN)
    for z in range(ZN):
        for x in range(XN):
            for c in range(CN):
                for y in range(YN):
                    at = dict(z=z, x=x, c=c, y=y)
                    to = dict(at)
                    to[axes[c]] = (at[axes[c]] + d) % size[axes[c]]
                    flat = [((p["z"] * XN + p["x"]) * CN + p["c"]) * YN + p["y"] for p in (at, to)]
                    pairs.append(tuple(flat))
    return pairs


def fetch(v, axes, d):
    return lax.ppermute(v, ALL, [(b, a) for a, b in shifted(axes, d)])


def give(v, axes, d):
    return lax.ppermute(v, ALL, shifted(axes, d))


def ring(v, axes):
    return [v] + [fetch(v, axes, d) for d in range(1, 4)]


def gathered_sum(v, axes):
    p = ring(v, axes)
    return (p[0] + p[2]) + (p[1] + p[3])


def returned(vs, axes):
    return [vs[0]] + [give(vs[d], axes, d) for d in range(1, len(vs))]


def steps(target_xyz, source_xyz, target_count, source_count, psi, omega):
    z, x, core, yq = (lax.axis_index(n) for n in ALL)
    along = jnp.where(core == 0, x, z)
    across = jnp.where(core == 0, z, x)
    where = jnp.stack([yq, target_count[0], source_count[0], core, along, across])
    where = where.astype(jnp.int32)
    tpay, spay = pack(where, target_xyz, source_xyz, psi, omega)
    trow = ring(tpay, FIRST)
    srow = ring(spay, SAME["y"])
    column = jnp.stack(trow)
    tin = [column]
    for d in (1, 2, 3):
        tin.append(fetch(column, LAST, d))
    sfar = [fetch(spay, SAME["c"], 1)]
    sfar += [fetch(v, SAME["c"], 1) for v in srow[1:]]
    src = sources([*srow, *sfar])
    y0, za = sketch(tin[0:1], src)
    y1, zb = sketch(tin[1:2], src)
    y3, zd = sketch(tin[3:4], src)
    y2, z0, z1 = sketch(tin[2:3], src, (za, zb, zd))
    ys = [y0, y1, y2, y3]
    zfar = give(z1, SAME["c"], 1)
    ys[1] = give(ys[1], LAST, 1)
    ys[3] = give(ys[3], LAST, 3)
    ys[2] = give(ys[2], LAST, 2)
    zmine = [z0[d] + zfar[d] for d in range(YN)]
    zs = returned(zmine, SAME["y"])
    ys = [(ys[0][d] + ys[1][d]) + (ys[2][d] + ys[3][d]) for d in range(ZN)]
    ys = returned(ys, FIRST)
    yfin, zfin, keep, send = finish(where, ys, zs, tpay)
    ys = ring(yfin, SAME["y"])
    half = keep + fetch(send, SAME["c"], 1)
    half = half.reshape(3, ZN, R // CN // ZN, R)
    chunks = [
        lax.dynamic_index_in_dim(half, lax.rem(along + d, ZN), 1, keepdims=False)
        for d in range(ZN)
    ]
    p = returned(chunks, FIRST)
    mine = (p[0] + p[1]) + (p[2] + p[3])
    mine = gathered_sum(mine, LAST)
    mine = gathered_sum(mine, SAME["y"])
    own = ring(mine, FIRST)
    other = fetch(jnp.stack(own), SAME["c"], 1)
    y, g0, g1, g2 = place(where, ys, own, other)
    return (y, zfin, g0, g1, g2)


def solution(mesh):
    grid = Mesh(mesh.devices.reshape(ZN, XN, CN, YN), ALL)
    pts = ("z", "x", "c")
    return jax.shard_map(
        steps,
        mesh=grid,
        in_specs=(P(None, pts), P(None, ALL), P(pts), P(ALL), P(pts, None), P(ALL, None)),
        out_specs=(P(pts, None), P(ALL, None), P(), P(), P()),
        check_vma=False,
    )
```

```python
import functools
import math

import jax
import jax.numpy as jnp
from jax import lax
from jax.experimental import pallas as pl
from jax.experimental.pallas import tpu as pltpu
from jax.sharding import Mesh, PartitionSpec as P


SHIFT = 1.05
SPREAD = 8.0
ZN, XN, CN, YN = 4, 4, 2, 4
ALL = ("z", "x", "c", "y")
R = 256
TCAP, SCAP = 1024, 512
TQ = TCAP // YN
GRAN = 16
NT = ZN * XN
NS = CN * YN
TC = 256
SC = 512
TPAY = TQ + 32
SPAY = SCAP + 64
FAR = 4.0
F32 = jnp.float32
BF16 = jnp.bfloat16


def inside(*arrays):
    return [pltpu.with_memory_space_constraint(v, pltpu.VMEM) for v in arrays]


def three_pieces(v):
    hi = v.astype(BF16)
    rest = v - hi.astype(F32)
    mid = rest.astype(BF16)
    low = (rest - mid.astype(F32)).astype(BF16)
    return hi, mid, low


def pack_kernel(where_ref, txyz_ref, sxyz_ref, psi_ref, omega_ref, tpay_ref, spay_ref, cols, quarter):
    yq = where_ref[0]
    tcount = where_ref[1]
    scount = where_ref[2]
    rows16 = lax.broadcasted_iota(jnp.int32, (GRAN, R), 0)
    cols[...] = jnp.concatenate(
        [txyz_ref[...], jnp.zeros((5, TCAP), F32)], axis=0
    ).T
    for a in range(TQ // GRAN):
        start = pl.multiple_of((a * YN + yq) * GRAN, GRAN)
        block = psi_ref[pl.ds(start, GRAN), :]
        tpay_ref[a * GRAN:(a + 1) * GRAN, :] = jnp.where(
            rows16 + start < tcount, block, jnp.zeros_like(block)
        )
        quarter[a * GRAN:(a + 1) * GRAN, :] = cols[pl.ds(start, GRAN), :]
    step = GRAN * YN
    tlive = (tcount // step) * GRAN + jnp.clip(tcount % step - yq * GRAN, 0, GRAN)
    sub = lax.broadcasted_iota(jnp.int32, (8, TQ), 0)
    tpos = quarter[...].T
    tpos = jnp.where((sub == 1) | (sub == 2), tpos * SPREAD, tpos)
    tpos = jnp.where(sub == 3, tlive.astype(F32), tpos)
    tail = jnp.zeros((8, R), BF16)
    tpay_ref[TQ:TPAY, :] = jnp.concatenate([*three_pieces(tpos), tail], axis=0)
    srow = lax.broadcasted_iota(jnp.int32, (SCAP, R), 0)
    om = omega_ref[...]
    spay_ref[0:SCAP, :] = jnp.where(srow < scount, om, jnp.zeros_like(om))
    for h in range(SCAP // R):
        part = jnp.concatenate(
            [sxyz_ref[:, h * R:(h + 1) * R], jnp.zeros((5, R), F32)], axis=0
        )
        part = jnp.where((sub == 1) | (sub == 2), part * SPREAD, part)
        part = jnp.where(sub == 0, part + SHIFT, part)
        part = jnp.where(sub == 3, (scount - h * R).clip(0, R).astype(F32), part)
        base = SCAP + 32 * h
        spay_ref[base:base + 32, :] = jnp.concatenate([*three_pieces(part), tail], axis=0)


def pack(where, txyz, sxyz, psi, omega):
    vm = pl.BlockSpec(memory_space=pltpu.VMEM)
    return pl.pallas_call(
        pack_kernel,
        out_shape=(
            jax.ShapeDtypeStruct((TPAY, R), BF16),
            jax.ShapeDtypeStruct((SPAY, R), BF16),
        ),
        in_specs=[pl.BlockSpec(memory_space=pltpu.SMEM), vm, vm, vm, vm],
        out_specs=(vm, vm),
        scratch_shapes=[pltpu.VMEM((TCAP, 8), F32), pltpu.VMEM((TQ, 8), F32)],
    )(where, txyz, sxyz, psi, omega)


def join(ref, *at):
    lo = at[-1]
    lead = at[:-1]
    v = ref[(*lead, slice(lo, lo + 32), slice(None))].astype(F32)
    return v[0:8] + v[8:16] + v[16:24]


def ceil16(n):
    return ((n + GRAN - 1) // GRAN) * GRAN


TROWS = 2 * TC
SROWS = NS * SCAP + 2 * SC


def first_lane(row):
    return jnp.max(row).astype(jnp.int32)


def offsets(counts):
    off = [jnp.int32(0)]
    for n in counts:
        off.append(off[-1] + ceil16(n))
    return [pl.multiple_of(v, GRAN) for v in off]


def sources_kernel(*refs):
    sin, (omc, srow, scnt, spos) = refs[:NS], refs[NS:]
    counts = []
    for k in range(NS):
        both = [join(sin[k], SCAP + 32 * h)[3:4, 0:128] for h in range(SCAP // R)]
        scnt[k:k + 1, :] = sum(both)
        counts.append(first_lane(sum(both)))
    soff = offsets(counts)
    chunks = (soff[NS] + SC - 1) // SC
    scnt[NS:NS + 1, :] = jnp.full((1, 128), chunks.astype(F32))
    for k in range(NS):
        omc[pl.ds(soff[k], SCAP), :] = sin[k][0:SCAP, :]
        for h in range(SCAP // R):
            spos[pl.ds(soff[k] + h * R, R), :] = join(sin[k], SCAP + 32 * h).T
    omc[pl.ds(soff[NS], SC), :] = jnp.zeros((SC, R), BF16)
    spos[pl.ds(soff[NS], SC), :] = jnp.full((SC, 8), FAR, F32)

    def prepare(si, carry):
        srow[si] = spos[pl.ds(pl.multiple_of(si * SC, SC), SC), :].T
        return carry

    lax.fori_loop(0, chunks, prepare, 0)


def sources(sin):
    vm = pl.BlockSpec(memory_space=pltpu.VMEM)
    return pl.pallas_call(
        sources_kernel,
        out_shape=(
            jax.ShapeDtypeStruct((SROWS, R), BF16),
            jax.ShapeDtypeStruct((SROWS // SC, 8, SC), F32),
            jax.ShapeDtypeStruct((2 * NS, 128), F32),
        ),
        in_specs=[vm] * NS,
        out_specs=(vm,) * 3,
        scratch_shapes=[
            pltpu.VMEM((SROWS, 8), F32),
        ],
        compiler_params=pltpu.CompilerParams(vmem_limit_bytes=5 << 20),
    )(pltpu.with_memory_space_constraint(sin[0], pltpu.HBM), *inside(*sin[1:]))


def sketch_kernel(m, last, *refs):
    groups = m * ZN
    tin, refs = refs[:m], refs[m:]
    omc, srow, scnt = refs[:3]
    refs = refs[3:]
    if last:
        earlier, refs = refs[0], refs[1:]
    youts, refs = refs[:m], refs[m:]
    if last:
        zouts, refs = refs[:2], refs[2:]
        psic, tpos, bcx, bcy, bcz, yc, tile0, tile1, zc = refs
    else:
        zc, psic, tpos, bcx, bcy, bcz, yc, tile0, tile1 = refs
    ns = first_lane(scnt[NS:NS + 1, :])
    toff = offsets(
        [first_lane(join(tin[k // ZN], k % ZN, TQ)[3:4, 0:128]) for k in range(groups)]
    )
    for k in range(groups):
        ref, d = tin[k // ZN], k % ZN
        psic[pl.ds(toff[k], TQ), :] = ref[d, 0:TQ, :]
        tpos[pl.ds(toff[k], TQ), :] = join(ref, d, TQ).T
    psic[pl.ds(toff[groups], 2 * TC), :] = jnp.zeros((2 * TC, R), BF16)
    tpos[pl.ds(toff[groups], 2 * TC), :] = jnp.zeros((2 * TC, 8), F32)
    nt = (toff[groups] + TC - 1) // TC

    def clear(si, carry):
        zc[pl.ds(pl.multiple_of(si * SC, SC), SC), :] = jnp.zeros((SC, R), F32)
        return carry

    lax.fori_loop(0, ns, clear, 0)

    def columns(ti, carry):
        ta = pl.multiple_of(ti * TC, TC)
        tp = tpos[pl.ds(ta, TC), :]
        bcx[ti] = jnp.broadcast_to(tp[:, 0:1], (TC, 128))
        bcy[ti] = jnp.broadcast_to(tp[:, 1:2], (TC, 128))
        bcz[ti] = jnp.broadcast_to(tp[:, 2:3], (TC, 128))
        yc[pl.ds(ta, TC), :] = jnp.zeros((TC, R), F32)
        return carry

    lax.fori_loop(0, nt + 1, columns, 0)

    def make(at, tile):
        ti, si = at
        for j in range(SC // 128):
            lanes = slice(j * 128, (j + 1) * 128)
            dx = bcx[ti] - srow[si, 0:1, lanes]
            dy = bcy[ti] - srow[si, 1:2, lanes]
            dz = bcz[ti] - srow[si, 2:3, lanes]
            tile[:, lanes] = lax.rsqrt(dx * dx + dy * dy + dz * dz).astype(BF16)

    def use(at, tile):
        ta = pl.multiple_of(at[0] * TC, TC)
        sa = pl.multiple_of(at[1] * SC, SC)
        block = tile[...]
        yc[pl.ds(ta, TC), :] += jnp.dot(
            block, omc[pl.ds(sa, SC), :], preferred_element_type=F32
        )
        zc[pl.ds(sa, SC), :] += lax.dot_general(
            block, psic[pl.ds(ta, TC), :], (((0,), (0,)), ((), ())),
            preferred_element_type=F32,
        )

    def after(at):
        wrap = at[1] + 1 == ns
        return jnp.where(wrap, at[0] + 1, at[0]), jnp.where(wrap, 0, at[1] + 1)

    start = (jnp.int32(0), jnp.int32(0))
    make(start, tile0)

    def two_steps(p, first):
        second = after(first)
        use(first, tile0)
        make(second, tile1)
        third = after(second)
        use(second, tile1)
        make(third, tile0)
        return third

    lax.fori_loop(0, (nt * ns + 1) // 2, two_steps, start)
    for k in range(groups):
        youts[k // ZN][k % ZN] = yc[pl.ds(toff[k], TQ), :]
    if last:
        soff = offsets([first_lane(scnt[k:k + 1, :]) for k in range(NS)])
        for k in range(NS):
            rows = pl.ds(soff[k], SCAP)
            zouts[k // YN][k % YN] = zc[rows, :] + earlier[rows, :]


def sketch(tin, src, earlier=None):
    m = len(tin)
    last = earlier is not None
    vm = pl.BlockSpec(memory_space=pltpu.VMEM)
    trows = m * ZN * TQ + TROWS
    ypart = jax.ShapeDtypeStruct((ZN, TQ, R), F32)
    zhalf = jax.ShapeDtypeStruct((YN, SCAP, R), F32)
    zall = (SROWS, R)
    outs = [ypart] * m + ([zhalf] * CN if last else [jax.ShapeDtypeStruct(zall, F32)])
    operands = [*tin, *src] + ([earlier] if last else [])
    column = pltpu.VMEM((trows // TC, TC, 128), F32)
    scratch = [
        pltpu.VMEM((trows, R), BF16),
        pltpu.VMEM((trows, 8), F32),
        column,
        column,
        column,
        pltpu.VMEM((trows, R), F32),
        pltpu.VMEM((TC, SC), BF16),
        pltpu.VMEM((TC, SC), BF16),
    ]
    return pl.pallas_call(
        functools.partial(sketch_kernel, m, last),
        out_shape=tuple(outs),
        in_specs=[vm] * len(operands),
        out_specs=(vm,) * len(outs),
        scratch_shapes=scratch + ([pltpu.VMEM(zall, F32)] if last else []),
        compiler_params=pltpu.CompilerParams(vmem_limit_bytes=(8 + 5 * m + 6 * last) << 20),
    )(*inside(*operands))


def finish_kernel(where_ref, y0, y1, y2, y3, z0, z1, z2, z3, tpay,
                  yfin_ref, zfin_ref, keep_ref, send_ref, *, yscale, zscale, tn, sn):
    yq, tcount, scount, core = where_ref[0], where_ref[1], where_ref[2], where_ref[3]
    q = lax.broadcasted_iota(jnp.int32, (TQ, R), 0)
    slot = (q // GRAN) * (GRAN * YN) + yq * GRAN + q % GRAN
    total = (y0[...] + y1[...]) + (y2[...] + y3[...])
    yfin_ref[...] = jnp.where(slot < tcount, total * yscale, 0.0)
    srow = lax.broadcasted_iota(jnp.int32, (SCAP, R), 0)
    total = (z0[...] + z1[...]) + (z2[...] + z3[...])
    zfin_ref[...] = jnp.where(srow < scount, total * zscale, 0.0)
    psi = tpay[0:TQ, :].astype(F32)
    y, z = yfin_ref[...], zfin_ref[...]
    hi = lax.Precision.HIGHEST
    dims = (((0,), (0,)), ((), ()))
    parts = (
        lax.dot_general(psi, y, dims, precision=hi, preferred_element_type=F32) / math.sqrt(tn),
        lax.dot_general(y, y, dims, precision=hi, preferred_element_type=F32) / tn,
        lax.dot_general(z, z, dims, precision=hi, preferred_element_type=F32) / sn,
    )
    first = core == 0
    for k in range(3):
        top, low = parts[k][0:R // 2, :], parts[k][R // 2:, :]
        keep_ref[k] = jnp.where(first, top, low)
        send_ref[k] = jnp.where(first, low, top)


def finish(where, y, z, tpay):
    tn, sn = TCAP * NT * CN, SCAP * NT * NS
    vm = pl.BlockSpec(memory_space=pltpu.VMEM)
    half = jax.ShapeDtypeStruct((3, R // 2, R), F32)

    def body(*refs):
        finish_kernel(
            *refs, yscale=2.0 / math.sqrt(sn), zscale=2.0 / math.sqrt(tn), tn=tn, sn=sn
        )

    return pl.pallas_call(
        body,
        out_shape=(
            jax.ShapeDtypeStruct((TQ, R), F32),
            jax.ShapeDtypeStruct((SCAP, R), F32),
            half,
            half,
        ),
        in_specs=[pl.BlockSpec(memory_space=pltpu.SMEM)] + [vm] * 9,
        out_specs=(vm,) * 4,
        compiler_params=pltpu.CompilerParams(vmem_limit_bytes=14 << 20),
    )(where, *inside(*y, *z, tpay))


def place_kernel(where_ref, *refs):
    ys, own, other = refs[0:YN], refs[YN:YN + ZN], refs[YN + ZN]
    yout, outs = refs[YN + ZN + 1], refs[YN + ZN + 2:]
    yq, core = where_ref[0], where_ref[3]
    for d in range(YN):
        q = lax.rem(yq + d, YN)
        for a in range(TQ // GRAN):
            at = pl.multiple_of((a * YN + q) * GRAN, GRAN)
            yout[pl.ds(at, GRAN), :] = ys[d][a * GRAN:(a + 1) * GRAN, :]
    share = R // CN // ZN
    for d in range(ZN):
        q = lax.rem(where_ref[4] + d, ZN)
        at = pl.multiple_of((core * ZN + q) * share, share)
        q = lax.rem(where_ref[5] + d, ZN)
        far = pl.multiple_of(((1 - core) * ZN + q) * share, share)
        for k in range(3):
            outs[k][pl.ds(at, share), :] = own[d][k]
            outs[k][pl.ds(far, share), :] = other[d, k]


def place(where, ys, own, other):
    vm = pl.BlockSpec(memory_space=pltpu.VMEM)
    return pl.pallas_call(
        place_kernel,
        out_shape=(
            jax.ShapeDtypeStruct((TCAP, R), F32),
            *[jax.ShapeDtypeStruct((R, R), F32)] * 3,
        ),
        in_specs=[pl.BlockSpec(memory_space=pltpu.SMEM)] + [vm] * (YN + ZN + 1),
        out_specs=(vm,) * 4,
        compiler_params=pltpu.CompilerParams(vmem_limit_bytes=10 << 20),
    )(where, *inside(*ys, *own, other))


FIRST = ("x", "z")
LAST = ("z", "x")
SAME = {name: (name, name) for name in ALL}


def shifted(axes, d):
    pairs = []
    size = dict(z=ZN, x=XN, c=CN, y=YN)
    for z in range(ZN):
        for x in range(XN):
            for c in range(CN):
                for y in range(YN):
                    at = dict(z=z, x=x, c=c, y=y)
                    to = dict(at)
                    to[axes[c]] = (at[axes[c]] + d) % size[axes[c]]
                    flat = [((p["z"] * XN + p["x"]) * CN + p["c"]) * YN + p["y"] for p in (at, to)]
                    pairs.append(tuple(flat))
    return pairs


def fetch(v, axes, d):
    return lax.ppermute(v, ALL, [(b, a) for a, b in shifted(axes, d)])


def give(v, axes, d):
    return lax.ppermute(v, ALL, shifted(axes, d))


def ring(v, axes):
    return [v] + [fetch(v, axes, d) for d in range(1, 4)]


def gathered_sum(v, axes):
    p = ring(v, axes)
    return (p[0] + p[2]) + (p[1] + p[3])


def returned(vs, axes):
    return [vs[0]] + [give(vs[d], axes, d) for d in range(1, len(vs))]


def steps(target_xyz, source_xyz, target_count, source_count, psi, omega):
    z, x, core, yq = (lax.axis_index(n) for n in ALL)
    along = jnp.where(core == 0, x, z)
    across = jnp.where(core == 0, z, x)
    where = jnp.stack([yq, target_count[0], source_count[0], core, along, across])
    where = where.astype(jnp.int32)
    tpay, spay = pack(where, target_xyz, source_xyz, psi, omega)
    trow = ring(tpay, FIRST)
    srow = ring(spay, SAME["y"])
    column = jnp.stack(trow)
    tin = [column]
    for d in (1, 2, 3):
        tin.append(fetch(column, LAST, d))
    sfar = [fetch(spay, SAME["c"], 1)]
    sfar += [fetch(v, SAME["c"], 1) for v in srow[1:]]
    src = sources([*srow, *sfar])
    y0, y3, za = sketch([tin[0], tin[3]], src)
    y2, y1, z0, z1 = sketch([tin[2], tin[1]], src, za)
    ys = [y0, y1, y2, y3]
    zfar = give(z1, SAME["c"], 1)
    ys[3] = give(ys[3], LAST, 3)
    ys[2] = give(ys[2], LAST, 2)
    ys[1] = give(ys[1], LAST, 1)
    zmine = [z0[d] + zfar[d] for d in range(YN)]
    zs = returned(zmine, SAME["y"])
    ys = [(ys[0][d] + ys[1][d]) + (ys[2][d] + ys[3][d]) for d in range(ZN)]
    ys = returned(ys, FIRST)
    yfin, zfin, keep, send = finish(where, ys, zs, tpay)
    ys = ring(yfin, SAME["y"])
    half = keep + fetch(send, SAME["c"], 1)
    half = half.reshape(3, ZN, R // CN // ZN, R)
    chunks = [
        lax.dynamic_index_in_dim(half, lax.rem(along + d, ZN), 1, keepdims=False)
        for d in range(ZN)
    ]
    p = returned(chunks, FIRST)
    mine = (p[0] + p[1]) + (p[2] + p[3])
    mine = gathered_sum(mine, LAST)
    mine = gathered_sum(mine, SAME["y"])
    own = ring(mine, FIRST)
    other = fetch(jnp.stack(own), SAME["c"], 1)
    y, g0, g1, g2 = place(where, ys, own, other)
    return (y, zfin, g0, g1, g2)


def solution(mesh):
    grid = Mesh(mesh.devices.reshape(ZN, XN, CN, YN), ALL)
    pts = ("z", "x", "c")
    return jax.shard_map(
        steps,
        mesh=grid,
        in_specs=(P(None, pts), P(None, ALL), P(pts), P(ALL), P(pts, None), P(ALL, None)),
        out_specs=(P(pts, None), P(ALL, None), P(), P(), P()),
        check_vma=False,
    )
```

```python
import functools
import math

import jax
import jax.numpy as jnp
from jax import lax
from jax.experimental import pallas as pl
from jax.experimental.pallas import tpu as pltpu
from jax.sharding import Mesh, PartitionSpec as P


SHIFT = 1.05
SPREAD = 8.0
ZN, XN, CN, YN = 4, 4, 2, 4
ALL = ("z", "x", "c", "y")
R = 256
TCAP, SCAP = 1024, 512
TQ = TCAP // YN
GRAN = 16
NT = ZN * XN
NS = CN * YN
TC = 256
SC = 512
TPAY = TQ + 32
SPAY = SCAP + 64
FAR = 4.0
F32 = jnp.float32
BF16 = jnp.bfloat16


def inside(*arrays):
    return [pltpu.with_memory_space_constraint(v, pltpu.VMEM) for v in arrays]


def three_pieces(v):
    hi = v.astype(BF16)
    rest = v - hi.astype(F32)
    mid = rest.astype(BF16)
    low = (rest - mid.astype(F32)).astype(BF16)
    return hi, mid, low


def pack_kernel(where_ref, txyz_ref, sxyz_ref, psi_ref, omega_ref, tpay_ref, spay_ref, cols, quarter):
    yq = where_ref[0]
    tcount = where_ref[1]
    scount = where_ref[2]
    rows16 = lax.broadcasted_iota(jnp.int32, (GRAN, R), 0)
    cols[...] = jnp.concatenate(
        [txyz_ref[...], jnp.zeros((5, TCAP), F32)], axis=0
    ).T
    for a in range(TQ // GRAN):
        start = pl.multiple_of((a * YN + yq) * GRAN, GRAN)
        block = psi_ref[pl.ds(start, GRAN), :]
        tpay_ref[a * GRAN:(a + 1) * GRAN, :] = jnp.where(
            rows16 + start < tcount, block, jnp.zeros_like(block)
        )
        quarter[a * GRAN:(a + 1) * GRAN, :] = cols[pl.ds(start, GRAN), :]
    step = GRAN * YN
    tlive = (tcount // step) * GRAN + jnp.clip(tcount % step - yq * GRAN, 0, GRAN)
    sub = lax.broadcasted_iota(jnp.int32, (8, TQ), 0)
    tpos = quarter[...].T
    tpos = jnp.where((sub == 1) | (sub == 2), tpos * SPREAD, tpos)
    tpos = jnp.where(sub == 3, tlive.astype(F32), tpos)
    tail = jnp.zeros((8, R), BF16)
    tpay_ref[TQ:TPAY, :] = jnp.concatenate([*three_pieces(tpos), tail], axis=0)
    srow = lax.broadcasted_iota(jnp.int32, (SCAP, R), 0)
    om = omega_ref[...]
    spay_ref[0:SCAP, :] = jnp.where(srow < scount, om, jnp.zeros_like(om))
    for h in range(SCAP // R):
        part = jnp.concatenate(
            [sxyz_ref[:, h * R:(h + 1) * R], jnp.zeros((5, R), F32)], axis=0
        )
        part = jnp.where((sub == 1) | (sub == 2), part * SPREAD, part)
        part = jnp.where(sub == 0, part + SHIFT, part)
        part = jnp.where(sub == 3, (scount - h * R).clip(0, R).astype(F32), part)
        base = SCAP + 32 * h
        spay_ref[base:base + 32, :] = jnp.concatenate([*three_pieces(part), tail], axis=0)


def pack(where, txyz, sxyz, psi, omega):
    vm = pl.BlockSpec(memory_space=pltpu.VMEM)
    return pl.pallas_call(
        pack_kernel,
        out_shape=(
            jax.ShapeDtypeStruct((TPAY, R), BF16),
            jax.ShapeDtypeStruct((SPAY, R), BF16),
        ),
        in_specs=[pl.BlockSpec(memory_space=pltpu.SMEM), vm, vm, vm, vm],
        out_specs=(vm, vm),
        scratch_shapes=[pltpu.VMEM((TCAP, 8), F32), pltpu.VMEM((TQ, 8), F32)],
    )(where, txyz, sxyz, psi, omega)


def join(ref, *at):
    lo = at[-1]
    lead = at[:-1]
    v = ref[(*lead, slice(lo, lo + 32), slice(None))].astype(F32)
    return v[0:8] + v[8:16] + v[16:24]


def ceil16(n):
    return ((n + GRAN - 1) // GRAN) * GRAN


TROWS = 2 * TC
SROWS = NS * SCAP + 2 * SC


def first_lane(row):
    return jnp.max(row).astype(jnp.int32)


def offsets(counts):
    off = [jnp.int32(0)]
    for n in counts:
        off.append(off[-1] + ceil16(n))
    return [pl.multiple_of(v, GRAN) for v in off]


def sources_kernel(*refs):
    sin, (omc, srow, scnt, spos) = refs[:NS], refs[NS:]
    counts = []
    for k in range(NS):
        both = [join(sin[k], SCAP + 32 * h)[3:4, 0:128] for h in range(SCAP // R)]
        scnt[k:k + 1, :] = sum(both)
        counts.append(first_lane(sum(both)))
    soff = offsets(counts)
    chunks = (soff[NS] + SC - 1) // SC
    scnt[NS:NS + 1, :] = jnp.full((1, 128), chunks.astype(F32))
    for k in range(NS):
        omc[pl.ds(soff[k], SCAP), :] = sin[k][0:SCAP, :]
        for h in range(SCAP // R):
            spos[pl.ds(soff[k] + h * R, R), :] = join(sin[k], SCAP + 32 * h).T
    omc[pl.ds(soff[NS], SC), :] = jnp.zeros((SC, R), BF16)
    spos[pl.ds(soff[NS], SC), :] = jnp.full((SC, 8), FAR, F32)

    def prepare(si, carry):
        srow[si] = spos[pl.ds(pl.multiple_of(si * SC, SC), SC), :].T
        return carry

    lax.fori_loop(0, chunks, prepare, 0)


def sources(sin):
    vm = pl.BlockSpec(memory_space=pltpu.VMEM)
    return pl.pallas_call(
        sources_kernel,
        out_shape=(
            jax.ShapeDtypeStruct((SROWS, R), BF16),
            jax.ShapeDtypeStruct((SROWS // SC, 8, SC), F32),
            jax.ShapeDtypeStruct((2 * NS, 128), F32),
        ),
        in_specs=[vm] * NS,
        out_specs=(vm,) * 3,
        scratch_shapes=[
            pltpu.VMEM((SROWS, 8), F32),
        ],
        compiler_params=pltpu.CompilerParams(vmem_limit_bytes=5 << 20),
    )(pltpu.with_memory_space_constraint(sin[0], pltpu.HBM), *inside(*sin[1:]))


def sketch_kernel(m, last, *refs):
    groups = m * ZN
    tin, refs = refs[:m], refs[m:]
    omc, srow, scnt = refs[:3]
    refs = refs[3:]
    if last:
        earlier, refs = refs[:3], refs[3:]
    youts, refs = refs[:m], refs[m:]
    if last:
        zouts, refs = refs[:2], refs[2:]
        psic, tpos, bcx, bcy, bcz, yc, tile0, tile1, zc = refs
    else:
        zc, psic, tpos, bcx, bcy, bcz, yc, tile0, tile1 = refs
    ns = first_lane(scnt[NS:NS + 1, :])
    toff = offsets(
        [first_lane(join(tin[k // ZN], k % ZN, TQ)[3:4, 0:128]) for k in range(groups)]
    )
    for k in range(groups):
        ref, d = tin[k // ZN], k % ZN
        psic[pl.ds(toff[k], TQ), :] = ref[d, 0:TQ, :]
        tpos[pl.ds(toff[k], TQ), :] = join(ref, d, TQ).T
    psic[pl.ds(toff[groups], 2 * TC), :] = jnp.zeros((2 * TC, R), BF16)
    tpos[pl.ds(toff[groups], 2 * TC), :] = jnp.zeros((2 * TC, 8), F32)
    nt = (toff[groups] + TC - 1) // TC

    def clear(si, carry):
        zc[pl.ds(pl.multiple_of(si * SC, SC), SC), :] = jnp.zeros((SC, R), F32)
        return carry

    lax.fori_loop(0, ns, clear, 0)

    def columns(ti, carry):
        ta = pl.multiple_of(ti * TC, TC)
        tp = tpos[pl.ds(ta, TC), :]
        bcx[ti] = jnp.broadcast_to(tp[:, 0:1], (TC, 128))
        bcy[ti] = jnp.broadcast_to(tp[:, 1:2], (TC, 128))
        bcz[ti] = jnp.broadcast_to(tp[:, 2:3], (TC, 128))
        yc[pl.ds(ta, TC), :] = jnp.zeros((TC, R), F32)
        return carry

    lax.fori_loop(0, nt + 1, columns, 0)

    def make(at, tile):
        ti, si = at
        for j in range(SC // 128):
            lanes = slice(j * 128, (j + 1) * 128)
            dx = bcx[ti] - srow[si, 0:1, lanes]
            dy = bcy[ti] - srow[si, 1:2, lanes]
            dz = bcz[ti] - srow[si, 2:3, lanes]
            tile[:, lanes] = lax.rsqrt(dx * dx + dy * dy + dz * dz).astype(BF16)

    def use(at, tile):
        ta = pl.multiple_of(at[0] * TC, TC)
        sa = pl.multiple_of(at[1] * SC, SC)
        block = tile[...]
        yc[pl.ds(ta, TC), :] += jnp.dot(
            block, omc[pl.ds(sa, SC), :], preferred_element_type=F32
        )
        zc[pl.ds(sa, SC), :] += lax.dot_general(
            block, psic[pl.ds(ta, TC), :], (((0,), (0,)), ((), ())),
            preferred_element_type=F32,
        )

    def after(at):
        wrap = at[1] + 1 == ns
        return jnp.where(wrap, at[0] + 1, at[0]), jnp.where(wrap, 0, at[1] + 1)

    start = (jnp.int32(0), jnp.int32(0))
    make(start, tile0)

    def two_steps(p, first):
        second = after(first)
        use(first, tile0)
        make(second, tile1)
        third = after(second)
        use(second, tile1)
        make(third, tile0)
        return third

    lax.fori_loop(0, (nt * ns + 1) // 2, two_steps, start)
    for k in range(groups):
        youts[k // ZN][k % ZN] = yc[pl.ds(toff[k], TQ), :]
    if last:
        soff = offsets([first_lane(scnt[k:k + 1, :]) for k in range(NS)])
        for k in range(NS):
            rows = pl.ds(soff[k], SCAP)
            total = zc[rows, :] + earlier[2][rows, :]
            total = total + (earlier[0][rows, :] + earlier[1][rows, :])
            zouts[k // YN][k % YN] = total


def sketch(tin, src, earlier=None):
    m = len(tin)
    last = earlier is not None
    vm = pl.BlockSpec(memory_space=pltpu.VMEM)
    trows = m * ZN * TQ + TROWS
    ypart = jax.ShapeDtypeStruct((ZN, TQ, R), F32)
    zhalf = jax.ShapeDtypeStruct((YN, SCAP, R), F32)
    zall = (SROWS, R)
    outs = [ypart] * m + ([zhalf] * CN if last else [jax.ShapeDtypeStruct(zall, F32)])
    operands = [*tin, *src, *(earlier or ())]
    column = pltpu.VMEM((trows // TC, TC, 128), F32)
    scratch = [
        pltpu.VMEM((trows, R), BF16),
        pltpu.VMEM((trows, 8), F32),
        column,
        column,
        column,
        pltpu.VMEM((trows, R), F32),
        pltpu.VMEM((TC, SC), BF16),
        pltpu.VMEM((TC, SC), BF16),
    ]
    return pl.pallas_call(
        functools.partial(sketch_kernel, m, last),
        out_shape=tuple(outs),
        in_specs=[vm] * len(operands),
        out_specs=(vm,) * len(outs),
        scratch_shapes=scratch + ([pltpu.VMEM(zall, F32)] if last else []),
        compiler_params=pltpu.CompilerParams(vmem_limit_bytes=(8 + 5 * m + 6 * last) << 20),
    )(*inside(*operands))


def finish_kernel(where_ref, y0, y1, y2, y3, z0, z1, z2, z3, tpay,
                  yfin_ref, zfin_ref, keep_ref, send_ref, *, yscale, zscale, tn, sn):
    yq, tcount, scount, core = where_ref[0], where_ref[1], where_ref[2], where_ref[3]
    q = lax.broadcasted_iota(jnp.int32, (TQ, R), 0)
    slot = (q // GRAN) * (GRAN * YN) + yq * GRAN + q % GRAN
    total = (y0[...] + y1[...]) + (y2[...] + y3[...])
    yfin_ref[...] = jnp.where(slot < tcount, total * yscale, 0.0)
    srow = lax.broadcasted_iota(jnp.int32, (SCAP, R), 0)
    total = (z0[...] + z1[...]) + (z2[...] + z3[...])
    zfin_ref[...] = jnp.where(srow < scount, total * zscale, 0.0)
    psi = tpay[0:TQ, :].astype(F32)
    y, z = yfin_ref[...], zfin_ref[...]
    hi = lax.Precision.HIGHEST
    dims = (((0,), (0,)), ((), ()))
    parts = (
        lax.dot_general(psi, y, dims, precision=hi, preferred_element_type=F32) / math.sqrt(tn),
        lax.dot_general(y, y, dims, precision=hi, preferred_element_type=F32) / tn,
        lax.dot_general(z, z, dims, precision=hi, preferred_element_type=F32) / sn,
    )
    first = core == 0
    for k in range(3):
        top, low = parts[k][0:R // 2, :], parts[k][R // 2:, :]
        keep_ref[k] = jnp.where(first, top, low)
        send_ref[k] = jnp.where(first, low, top)


def finish(where, y, z, tpay):
    tn, sn = TCAP * NT * CN, SCAP * NT * NS
    vm = pl.BlockSpec(memory_space=pltpu.VMEM)
    half = jax.ShapeDtypeStruct((3, R // 2, R), F32)

    def body(*refs):
        finish_kernel(
            *refs, yscale=2.0 / math.sqrt(sn), zscale=2.0 / math.sqrt(tn), tn=tn, sn=sn
        )

    return pl.pallas_call(
        body,
        out_shape=(
            jax.ShapeDtypeStruct((TQ, R), F32),
            jax.ShapeDtypeStruct((SCAP, R), F32),
            half,
            half,
        ),
        in_specs=[pl.BlockSpec(memory_space=pltpu.SMEM)] + [vm] * 9,
        out_specs=(vm,) * 4,
        compiler_params=pltpu.CompilerParams(vmem_limit_bytes=14 << 20),
    )(where, *inside(*y, *z, tpay))


def place_kernel(where_ref, *refs):
    ys, own, other = refs[0:YN], refs[YN:YN + ZN], refs[YN + ZN:YN + 2 * ZN]
    yout, outs = refs[YN + 2 * ZN], refs[YN + 2 * ZN + 1:]
    yq, core = where_ref[0], where_ref[3]
    for d in range(YN):
        q = lax.rem(yq + d, YN)
        for a in range(TQ // GRAN):
            at = pl.multiple_of((a * YN + q) * GRAN, GRAN)
            yout[pl.ds(at, GRAN), :] = ys[d][a * GRAN:(a + 1) * GRAN, :]
    share = R // CN // ZN
    for d in range(ZN):
        q = lax.rem(where_ref[4] + d, ZN)
        at = pl.multiple_of((core * ZN + q) * share, share)
        q = lax.rem(where_ref[5] + d, ZN)
        far = pl.multiple_of(((1 - core) * ZN + q) * share, share)
        for k in range(3):
            outs[k][pl.ds(at, share), :] = own[d][k]
            outs[k][pl.ds(far, share), :] = other[d][k]


def place(where, ys, own, other):
    vm = pl.BlockSpec(memory_space=pltpu.VMEM)
    return pl.pallas_call(
        place_kernel,
        out_shape=(
            jax.ShapeDtypeStruct((TCAP, R), F32),
            *[jax.ShapeDtypeStruct((R, R), F32)] * 3,
        ),
        in_specs=[pl.BlockSpec(memory_space=pltpu.SMEM)] + [vm] * (YN + 2 * ZN),
        out_specs=(vm,) * 4,
        compiler_params=pltpu.CompilerParams(vmem_limit_bytes=10 << 20),
    )(where, *inside(*ys, *own, *other))


FIRST = ("x", "z")
LAST = ("z", "x")
SAME = {name: (name, name) for name in ALL}


def shifted(axes, d):
    pairs = []
    size = dict(z=ZN, x=XN, c=CN, y=YN)
    for z in range(ZN):
        for x in range(XN):
            for c in range(CN):
                for y in range(YN):
                    at = dict(z=z, x=x, c=c, y=y)
                    to = dict(at)
                    to[axes[c]] = (at[axes[c]] + d) % size[axes[c]]
                    flat = [((p["z"] * XN + p["x"]) * CN + p["c"]) * YN + p["y"] for p in (at, to)]
                    pairs.append(tuple(flat))
    return pairs


def fetch(v, axes, d):
    return lax.ppermute(v, ALL, [(b, a) for a, b in shifted(axes, d)])


def give(v, axes, d):
    return lax.ppermute(v, ALL, shifted(axes, d))


def ring(v, axes):
    return [v] + [fetch(v, axes, d) for d in range(1, 4)]


def gathered_sum(v, axes):
    p = ring(v, axes)
    return (p[0] + p[2]) + (p[1] + p[3])


def returned(vs, axes):
    return [vs[0]] + [give(vs[d], axes, d) for d in range(1, len(vs))]


def steps(target_xyz, source_xyz, target_count, source_count, psi, omega):
    z, x, core, yq = (lax.axis_index(n) for n in ALL)
    along = jnp.where(core == 0, x, z)
    across = jnp.where(core == 0, z, x)
    where = jnp.stack([yq, target_count[0], source_count[0], core, along, across])
    where = where.astype(jnp.int32)
    tpay, spay = pack(where, target_xyz, source_xyz, psi, omega)
    trow = ring(tpay, FIRST)
    srow = ring(spay, SAME["y"])
    column = jnp.stack(trow)
    tin = [column]
    for d in (1, 2, 3):
        tin.append(fetch(column, LAST, d))
    sfar = [fetch(spay, SAME["c"], 1)]
    sfar += [fetch(v, SAME["c"], 1) for v in srow[1:]]
    src = sources([*srow, *sfar])
    y0, za = sketch(tin[0:1], src)
    y1, zb = sketch(tin[1:2], src)
    y3, zd = sketch(tin[3:4], src)
    y2, z0, z1 = sketch(tin[2:3], src, (za, zb, zd))
    ys = [y0, y1, y2, y3]
    zfar = give(z1, SAME["c"], 1)
    ys[1] = give(ys[1], LAST, 1)
    ys[3] = give(ys[3], LAST, 3)
    ys[2] = give(ys[2], LAST, 2)
    zmine = [z0[d] + zfar[d] for d in range(YN)]
    zs = returned(zmine, SAME["y"])
    ys = [(ys[0][d] + ys[1][d]) + (ys[2][d] + ys[3][d]) for d in range(ZN)]
    ys = returned(ys, FIRST)
    yfin, zfin, keep, send = finish(where, ys, zs, tpay)
    ys = ring(yfin, SAME["y"])
    half = keep + fetch(send, SAME["c"], 1)
    half = half.reshape(3, ZN, R // CN // ZN, R)
    chunks = [
        lax.dynamic_index_in_dim(half, lax.rem(along + d, ZN), 1, keepdims=False)
        for d in range(ZN)
    ]
    p = returned(chunks, FIRST)
    mine = (p[0] + p[1]) + (p[2] + p[3])
    mine = gathered_sum(mine, LAST)
    mine = gathered_sum(mine, SAME["y"])
    own = ring(mine, FIRST)
    other = [fetch(v, SAME["c"], 1) for v in own]
    y, g0, g1, g2 = place(where, ys, own, other)
    return (y, zfin, g0, g1, g2)


def solution(mesh):
    grid = Mesh(mesh.devices.reshape(ZN, XN, CN, YN), ALL)
    pts = ("z", "x", "c")
    return jax.shard_map(
        steps,
        mesh=grid,
        in_specs=(P(None, pts), P(None, ALL), P(pts), P(ALL), P(pts, None), P(ALL, None)),
        out_specs=(P(pts, None), P(ALL, None), P(), P(), P()),
        check_vma=False,
    )
```
